128 devices in a mesh: rows: 32 (over y, z_lo, x), tm: 4 (over z_hi, core).
Axes of the slice: x: 4, y: 4, z: 4 (z_hi: 2, z_lo: 2; z = z_hi * 2 + z_lo), core: 2. Of those that a mesh axis runs over, the one named last changes fastest.
Arguments:
- raw_frames: bfloat16 [320, 256, 2048], P('tm', 'rows'), may hold values from -6 to 6
- dark_frame: float32 [256, 2048], P('rows'), may hold values from -0.5 to 0.5
- flat_field: float32 [256, 2048], P('rows'), may hold values from 0.5 to 1.5
- pixel_gain: float32 [256, 2048], P('rows'), may hold values from 0.1 to 1.9
- smoothing_kernel: float32 [5, 5], replicated, may hold values from 0.05 to 0.5
- bin_labels: int32 [256, 2048], P('rows'), may hold values from 0 to 71999
- lag_list: int32 [64], replicated, may hold values from 1 to 79, as said below
Outputs:
- correlation: float32 [4608000], P(('rows', 'tm'))
The draws below stay inside these ranges and needn't reach their ends.
Inputs may be any that keep to these rules, and one draw needn't show every extreme that they name: `lag_list`: 64 distinct lags in rising order; the first is 1 and the last 79.
All inputs are finite; a program needn't handle non-finite values.
Results may differ from the reference program's by a relative error of at most 0.0054.
Values may be sent and summed in bfloat16 or wider, within the bound.
A program may use at most 256 MiB of HBM per device.

```python
import math
import jax
import jax.numpy as jnp
from jax import lax

H_DEV = 8
W = 2048
F_DEV = 80
LAGS = 64
ROWS = 256
FRAMES = 320
BINS = 72000
N_ROWS = 32


def draw_lag_list(key, part):
    inner_lags = jax.random.permutation(key, F_DEV - 3)[:LAGS - 2].astype(jnp.int32) + 2
    end_lags = jnp.array([1, F_DEV - 1], dtype=jnp.int32)
    return jnp.sort(jnp.concatenate([end_lags, inner_lags]))


def place_ends(result, stream_key, least, top_value):
    index_at = [jax.random.randint(jax.random.fold_in(stream_key, axis), (), 0, length) for axis, length in enumerate(result.shape)]
    longest = result.shape.index(max(result.shape))
    neighbour = index_at[:longest] + [(index_at[longest] + 1) % result.shape[longest]] + index_at[longest + 1:]
    return result.at[tuple(index_at)].set(least).at[tuple(neighbour)].set(top_value)


def steps_of(rng, dims, split, smallest, largest):
    loudness = 1.0
    for axis_at, blocks in split:
        draws = jax.random.uniform(jax.random.fold_in(jax.random.fold_in(rng, 6), axis_at), (blocks,), jnp.float32, smallest / len(split), largest / len(split))
        loudness = loudness * jnp.repeat(jnp.exp(draws), dims[axis_at] // blocks).reshape((-1,) + (1,) * (len(dims) - 1 - axis_at))
    return loudness


def centred(stream_key, dims, scale, limit, pieces=(), kind=jnp.bfloat16):
    level = steps_of(stream_key, dims, pieces, -0.22, 0.18) if pieces else 1.0
    values = jax.random.normal(stream_key, dims, jnp.float32) * scale * level
    return jnp.minimum(jnp.maximum(values, -limit), limit).astype(kind)


def setup_inputs(seed: int = 0) -> dict:
    splits = jax.random.split(jax.random.key(seed), 8)
    raw_frames = centred(splits[0], (FRAMES, ROWS, W), 1.0, 6.0, ((0, 4), (1, 32)))
    dark_frame = centred(splits[1], (ROWS, W), 0.08, 0.5, ((0, 32),), jnp.float32)
    flat_field = jnp.clip(1.0 + 0.1 * jax.random.normal(splits[2], (ROWS, W), jnp.float32), 0.5, 1.5)
    pixel_gain = jnp.clip(1.0 + 0.18 * jax.random.normal(splits[3], (ROWS, W), jnp.float32), 0.1, 1.9)
    smoothing_kernel = jnp.clip(jnp.exp(jax.random.uniform(splits[4], (5, 5), jnp.float32, math.log(0.05), math.log(0.5))), 0.05, 0.5)
    bin_labels = place_ends(jax.random.randint(splits[5], (ROWS, W), 0, BINS), jax.random.fold_in(splits[5], 1), 0, BINS - 1).astype(jnp.int32)
    lag_list = draw_lag_list(jax.random.fold_in(splits[7], 71), 0)
    return {"raw_frames": raw_frames, "dark_frame": dark_frame, "flat_field": flat_field, "pixel_gain": pixel_gain, "smoothing_kernel": smoothing_kernel, "bin_labels": bin_labels, "lag_list": lag_list}


def shift_columns(values, offset):
    if offset == 0:
        return values
    zero_pad = jnp.zeros(values.shape[:-1] + (abs(offset),), values.dtype)
    if offset > 0:
        return jnp.concatenate([values[..., offset:], zero_pad], axis=-1)
    return jnp.concatenate([zero_pad, values[..., :offset]], axis=-1)


def smooth_rows(padded, kernel, row_count):
    running = jnp.zeros((padded.shape[0], row_count, padded.shape[2]), jnp.float32)
    for kernel_row in range(5):
        band_rows = padded[:, kernel_row:kernel_row + row_count, :].astype(jnp.float32)
        for kernel_col in range(5):
            running = running + kernel[kernel_row, kernel_col] * shift_columns(band_rows, kernel_col - 2)
    return running.astype(jnp.bfloat16)


def slab_rows(array, axis, slab_index):
    first_row = (slab_index * H_DEV).astype(jnp.int32)
    upper_rows = lax.dynamic_slice_in_dim(array, jnp.maximum(first_row - 2, 0).astype(jnp.int32), 2, axis)
    middle = lax.dynamic_slice_in_dim(array, first_row, H_DEV, axis)
    lower_rows = lax.dynamic_slice_in_dim(array, jnp.minimum(first_row + H_DEV, ROWS - 2).astype(jnp.int32), 2, axis)
    return jnp.concatenate([upper_rows, middle, lower_rows], axis)


def reference(raw_frames, dark_frame, flat_field, pixel_gain, smoothing_kernel, bin_labels, lag_list):
    divisor = FRAMES - lag_list.astype(jnp.float32)

    def one_slab(bin_table, slab_index):
        raw_slab = slab_rows(raw_frames, 1, slab_index)
        dark_slab = slab_rows(dark_frame, 0, slab_index)
        flat_slab = slab_rows(flat_field, 0, slab_index)
        gain_slab = slab_rows(pixel_gain, 0, slab_index)
        valid_top = (slab_index > 0).astype(jnp.float32) * jnp.ones((2,), jnp.float32)
        valid_low = (slab_index < N_ROWS - 1).astype(jnp.float32) * jnp.ones((2,), jnp.float32)
        validity = jnp.concatenate([valid_top, jnp.ones((H_DEV,), jnp.float32), valid_low])
        weighted = ((raw_slab.astype(jnp.float32) - dark_slab) * flat_slab * gain_slab * validity[None, :, None]).astype(jnp.bfloat16)
        smoothed = smooth_rows(weighted, smoothing_kernel, H_DEV)
        series = smoothed.astype(jnp.float32).reshape(FRAMES, H_DEV * W)
        spectrum = jnp.fft.rfft(series, n=2 * FRAMES, axis=0)
        power_sum = spectrum.real * spectrum.real + spectrum.imag * spectrum.imag
        autocorr = jnp.fft.irfft(power_sum, n=2 * FRAMES, axis=0)
        lagged = autocorr[lag_list] / divisor[:, None]
        first_row = (slab_index * H_DEV).astype(jnp.int32)
        label_slab = lax.dynamic_slice_in_dim(bin_labels, first_row, H_DEV, 0).reshape(-1)
        bin_table = bin_table.at[:, label_slab].add(lagged)
        return bin_table, None

    empty_table = jnp.zeros((LAGS, BINS), jnp.float32)
    summed, _ = lax.scan(one_slab, empty_table, jnp.arange(N_ROWS, dtype=jnp.int32))
    return summed.reshape(-1)
```

```python
import functools

import jax
import jax.numpy as jnp
import numpy as np
from jax import lax
from jax.experimental import pallas as pl
from jax.experimental.pallas import tpu as pltpu
from jax.sharding import PartitionSpec as P

F32 = jnp.float32
BF16 = jnp.bfloat16
MESH = pl.DeviceIdType.MESH
VMEM = pltpu.MemorySpace.VMEM
SMEM = pltpu.MemorySpace.SMEM

ROWS8 = 8
W = 2048
FB = 80
TM = 4
QUARTER = W // TM
FRAMES = FB * TM
LAGS = 64
HALF = 36000
BW = 1152
NB = 64
CAP = 128
NDFT = 400
FPAD = 208
MROWS = 80


def dft_tables():
    t = np.arange(FRAMES)
    f = np.arange(NDFT // 2 + 1)
    angle = 2 * np.pi * ((f[:, None] * t[None, :]) % NDFT) / NDFT
    forward = np.zeros((2 * FPAD, FRAMES), np.float64)
    forward[: f.size] = np.cos(angle)
    forward[FPAD : FPAD + f.size] = np.sin(angle)
    k = np.arange(80)
    back = np.zeros((80, FPAD), np.float64)
    fold = np.full(f.size, 2.0)
    fold[0] = fold[-1] = 1.0
    back[:, : f.size] = np.cos(2 * np.pi * ((k[:, None] * f[None, :]) % NDFT) / NDFT) * fold / NDFT

    def split(a):
        hi = a.astype(jnp.bfloat16)
        lo = (a - hi.astype(np.float64)).astype(jnp.bfloat16)
        return hi, lo

    return (*split(forward), *split(back))


def smooth_kernel(taps, before, here, after, out, wp):
    wp[0:2] = before[...]
    wp[2:10] = here[...]
    wp[10:12] = after[...]
    lane = lax.broadcasted_iota(jnp.int32, (16, 128), 1)
    chunks = W // 128

    def one(step, carry):
        fb = step // ROWS8
        i = step % ROWS8
        frames = pl.ds(pl.multiple_of(fb * 16, 16), 16)
        rolled = []
        for c in range(chunks):
            rows = [wp[i + a, frames, c * 128 : (c + 1) * 128].astype(F32) for a in range(5)]
            part = []
            for b in range(5):
                acc = rows[0] * taps[0, b]
                for a in range(1, 5):
                    acc = acc + rows[a] * taps[a, b]
                part.append(acc)
            rolled.append(
                (
                    pltpu.roll(part[0], 2, 1),
                    pltpu.roll(part[1], 1, 1),
                    part[2],
                    pltpu.roll(part[3], 127, 1),
                    pltpu.roll(part[4], 126, 1),
                )
            )
            if c >= 1:
                finish(out, i, frames, c - 1, rolled)
        finish(out, i, frames, chunks - 1, rolled)
        return carry

    def finish(out, i, frames, c, rolled):
        zero = jnp.zeros((16, 128), F32)
        left = rolled[c - 1] if c > 0 else (zero,) * 5
        right = rolled[c + 1] if c + 1 < chunks else (zero,) * 5
        mine = rolled[c]
        total = mine[2]
        total = total + jnp.where(lane >= 2, mine[0], left[0])
        total = total + jnp.where(lane >= 1, mine[1], left[1])
        total = total + jnp.where(lane < 127, mine[3], right[3])
        total = total + jnp.where(lane < 126, mine[4], right[4])
        out[i, frames, c * 128 : (c + 1) * 128] = total.astype(BF16)

    lax.fori_loop(0, (FB // 16) * ROWS8, one, 0)


def smooth(taps, before, here, after):
    return pl.pallas_call(
        smooth_kernel,
        out_shape=jax.ShapeDtypeStruct((ROWS8, FB, W), BF16),
        in_specs=[pl.BlockSpec(memory_space=SMEM)] + [pl.BlockSpec(memory_space=VMEM)] * 3,
        out_specs=pl.BlockSpec(memory_space=VMEM),
        scratch_shapes=[pltpu.VMEM((ROWS8 + 4, FB, W), BF16)],
        compiler_params=pltpu.CompilerParams(vmem_limit_bytes=40 << 20),
        name="smooth",
    )(taps, before, here, after)


def bucket_of(label):
    half = label >= HALF
    inside = jnp.where(half, label - HALF, label)
    quotient = lax.shift_right_logical(lax.shift_right_logical(inside, 7) * 57, 9)
    bucket = jnp.where(half, quotient + 32, quotient)
    return bucket, inside - quotient * BW


def slot_kernel(step_ref, labels, slots, high, low, rounds):
    tm = lax.axis_index("tm")
    cols = pl.ds(pl.multiple_of(tm * QUARTER, QUARTER), QUARTER)
    upper = (
        lax.broadcasted_iota(jnp.int32, (QUARTER, QUARTER), 0)
        <= lax.broadcasted_iota(jnp.int32, (QUARTER, QUARTER), 1)
    ).astype(F32).astype(BF16)
    which = lax.broadcasted_iota(jnp.int32, (NB, QUARTER), 0)
    carry = jnp.zeros((NB, 1), F32)
    first = step_ref[0, 0] * CAP
    for i in range(ROWS8):
        label = labels[i : i + 1, cols]
        bucket, local = bucket_of(label)
        hot = (which == bucket).astype(F32)
        count = jnp.dot(hot.astype(BF16), upper, preferred_element_type=F32) + carry
        rank = jnp.sum(hot * count, axis=0, keepdims=True).astype(jnp.int32) - 1 - first
        inside = (rank >= 0) & (rank < CAP)
        slots[i : i + 1, :] = jnp.where(inside, bucket * CAP + rank, NB * CAP)
        top = lax.shift_right_logical(local, 7)
        high[i : i + 1, :] = top.astype(F32)
        low[i : i + 1, :] = (local - top * 128).astype(F32)
        carry = count[:, QUARTER - 1 : QUARTER]
    most = jnp.max(carry, axis=0, keepdims=True)
    needed = lax.shift_right_logical(most.astype(jnp.int32) + (CAP - 1), 7).astype(F32)
    rounds[...] = jnp.broadcast_to(needed, (8, QUARTER))


def slot_tables(step, labels):
    small = jax.ShapeDtypeStruct((ROWS8, QUARTER), F32)
    return pl.pallas_call(
        slot_kernel,
        out_shape=(jax.ShapeDtypeStruct((ROWS8, QUARTER), jnp.int32), small, small, small),
        in_specs=[pl.BlockSpec(memory_space=SMEM), pl.BlockSpec(memory_space=VMEM)],
        out_specs=(pl.BlockSpec(memory_space=VMEM),) * 4,
        name="slots",
    )(step, labels)


def lag_kernel(slots, series, high, low, rounds, lag_rows, fhi, flo, bhi, blo, out, src, dst):
    lag = lag_rows[...]
    pick = (lag[:, :80] == lax.broadcasted_iota(jnp.int32, (LAGS, 80), 1)).astype(F32).astype(BF16)
    chi = jnp.dot(pick, bhi[...], preferred_element_type=F32).astype(BF16)
    clo = jnp.dot(pick, blo[...], preferred_element_type=F32).astype(BF16)
    scale = 1.0 / (FRAMES - lag[:, :1].astype(F32))
    sub = lax.broadcasted_iota(jnp.int32, (8, QUARTER), 0)

    def clear(j, carry):
        dst[pl.ds(pl.multiple_of(j * 128, 128), 128), :] = jnp.zeros((128, 128), F32)
        return carry

    lax.fori_loop(0, NB, clear, 0)

    def row(i, carry):
        s = series[i]
        x = jnp.dot(fhi[...], s, preferred_element_type=F32)
        x = x + jnp.dot(flo[...], s, preferred_element_type=F32)
        power = x[:FPAD] * x[:FPAD] + x[FPAD:] * x[FPAD:]
        phi = power.astype(BF16)
        plo = (power - phi.astype(F32)).astype(BF16)
        r = jnp.dot(chi, phi, preferred_element_type=F32)
        r = r + jnp.dot(chi, plo, preferred_element_type=F32)
        r = r + jnp.dot(clo, phi, preferred_element_type=F32)
        r = r * scale
        mine = pl.ds(i, 1)
        extra = jnp.where(
            sub == 0,
            high[mine, :],
            jnp.where(sub == 1, low[mine, :], jnp.where(sub == 2, rounds[mine, :], 0.0)),
        )
        full = jnp.concatenate([r, extra, jnp.zeros((56, QUARTER), F32)], axis=0)
        src[pl.ds(pl.multiple_of(i * QUARTER, QUARTER), QUARTER), :] = full.T
        return carry

    lax.fori_loop(0, ROWS8, row, 0)

    per = 16

    def move(g, carry):
        i = g // (QUARTER // per)
        c = (g % (QUARTER // per)) * per
        base = pl.multiple_of(g * per, per)
        for u in range(per):
            to = slots[i, c + u]
            dst[pl.ds(to, 1), :] = src[pl.ds(base + u, 1), :]
        return carry

    lax.fori_loop(0, ROWS8 * QUARTER // per, move, 0)

    def turn(j, carry):
        block = dst[pl.ds(pl.multiple_of(j * 128, 128), 128), :].T
        out[j] = block[:MROWS].astype(BF16)
        return carry

    lax.fori_loop(0, NB, turn, 0)


def lag_messages(slots, series, high, low, rounds, lag_rows, tables):
    return pl.pallas_call(
        lag_kernel,
        out_shape=jax.ShapeDtypeStruct((NB, MROWS, CAP), BF16),
        in_specs=[pl.BlockSpec(memory_space=SMEM)] + [pl.BlockSpec(memory_space=VMEM)] * 9,
        out_specs=pl.BlockSpec(memory_space=VMEM),
        scratch_shapes=[
            pltpu.VMEM((ROWS8 * QUARTER, 128), F32),
            pltpu.VMEM((NB * CAP + 8, 128), F32),
        ],
        compiler_params=pltpu.CompilerParams(vmem_limit_bytes=40 << 20),
        name="lags",
    )(slots, series, high, low, rounds, lag_rows, *tables)


def position():
    rows = lax.axis_index("rows")
    tm = lax.axis_index("tm")
    y = rows // 8
    z = (tm // 2) * 2 + (rows // 4) % 2
    x = rows % 4
    return x, y, z, tm % 2


def at_offset(i, sign):
    x, y, z, _ = position()
    x = (x + sign * (i % 4) + 4) % 4
    y = (y + sign * ((i // 4) % 4) + 4) % 4
    z = (z + sign * (i // 16) + 4) % 4
    rows = y * 8 + (z % 2) * 4 + x
    return rows, z // 2


def bin_kernel(msgs, out, most, recv, acc, tops, fin, got, send_sem, recv_sem, fsend, frecv):
    rows_me = lax.axis_index("rows")
    tm_me = lax.axis_index("tm")
    core = tm_me % 2
    chip = rows_me * 2 + tm_me // 2

    barrier = pltpu.get_barrier_semaphore()

    def greet(i, carry):
        rows, zh = at_offset(i, 1)
        for c in range(2):

            @pl.when((i != 0) | (c != core))
            def _():
                pl.semaphore_signal(barrier, inc=1, device_id=(rows, zh * 2 + c), device_id_type=MESH)

        return carry

    lax.fori_loop(0, NB, greet, 0)
    pl.semaphore_wait(barrier, 2 * NB - 1)

    def route(i, sign):
        rows, zh = at_offset(i, sign)
        there = rows * 2 + zh
        return pltpu.make_async_remote_copy(
            src_ref=msgs.at[there],
            dst_ref=recv.at[i],
            send_sem=send_sem.at[i],
            recv_sem=recv_sem.at[i],
            device_id=(rows, zh * 2 + core),
            device_id_type=MESH,
        )

    def send(i, carry):
        route(i, 1).start()
        return carry

    lax.fori_loop(1, NB, send, 0)

    acc[...] = jnp.zeros_like(acc)
    tops[...] = jnp.zeros_like(tops)
    row_id = lax.broadcasted_iota(jnp.int32, (128, 2 * CAP), 0).astype(F32)

    def add(first, second):
        both = jnp.concatenate([first, second], axis=1)
        values = both[:LAGS]
        extra = both[LAGS : LAGS + 16].astype(F32)
        high, low = extra[0:1], extra[1:2]
        tops[...] = jnp.maximum(tops[...], extra[2:3])
        for h in range(BW // 128):
            key = jnp.where(high == h, low, -1.0)
            hot = jnp.where(row_id == key, 1.0, 0.0).astype(BF16)
            acc[:, h * 128 : (h + 1) * 128] += lax.dot_general(
                values, hot, (((1,), (1,)), ((), ())), preferred_element_type=F32
            )

    route(1, 1).wait_recv()
    add(msgs[chip], recv[1])

    def pair(g, carry):
        i = 2 * g
        route(i, 1).wait_recv()
        route(i + 1, 1).wait_recv()
        add(recv[i], recv[i + 1])
        return carry

    lax.fori_loop(1, NB // 2, pair, 0)

    for h in range(BW // 128):
        fin[:, h, :] = acc[:, h * 128 : (h + 1) * 128]
    peak = jnp.max(tops[...], axis=1, keepdims=True)
    fin[:, BW // 128, :] = jnp.broadcast_to(peak, (LAGS, 128))

    half = chip // 32
    place = core * 32 + chip % 32

    def owner(i):
        rows, zh = at_offset(i, 1)
        there = rows * 2 + zh
        return pltpu.make_async_remote_copy(
            src_ref=fin.at[there],
            dst_ref=got.at[place],
            send_sem=fsend.at[i],
            recv_sem=frecv.at[place],
            device_id=(rows, zh * 2 + half),
            device_id_type=MESH,
        )

    def hand(i, carry):
        owner(i).start()
        return carry

    lax.fori_loop(1, NB, hand, 0)

    own = pltpu.make_async_copy(fin.at[chip], got.at[place], frecv.at[place])

    @pl.when(half == core)
    def _():
        own.start()

    @pl.when(half != core)
    def _():
        owner(0).start()

    def arrived(n, carry):
        pltpu.make_async_copy(got.at[n], got.at[n], frecv.at[n]).wait()
        return carry

    lax.fori_loop(0, NB, arrived, 0)

    top = jnp.zeros((1, 128), F32)
    for j in range(32):
        out[9 * j : 9 * j + 9, :] = got[j, 0:9, :] + got[32 + j, 0:9, :]
        top = jnp.maximum(top, jnp.maximum(got[j, 9:10, :], got[32 + j, 9:10, :]))
    most[...] = jnp.broadcast_to(top, (8, 128))

    def drain(i, carry):
        route(i, 1).wait_send()
        owner(i).wait_send()
        return carry

    lax.fori_loop(1, NB, drain, 0)

    @pl.when(half != core)
    def _():
        owner(0).wait_send()


def bin_sums(msgs):
    return pl.pallas_call(
        bin_kernel,
        out_shape=(
            jax.ShapeDtypeStruct((32 * BW // 128, 128), F32),
            jax.ShapeDtypeStruct((8, 128), F32),
        ),
        in_specs=[pl.BlockSpec(memory_space=VMEM)],
        out_specs=(pl.BlockSpec(memory_space=VMEM),) * 2,
        scratch_shapes=[
            pltpu.VMEM((NB, MROWS, CAP), BF16),
            pltpu.VMEM((LAGS, BW), F32),
            pltpu.VMEM((1, 2 * CAP), F32),
            pltpu.VMEM((LAGS, BW // 128 + 1, 128), F32),
            pltpu.VMEM((NB, BW // 128 + 1, 128), F32),
            pltpu.SemaphoreType.DMA((NB,)),
            pltpu.SemaphoreType.DMA((NB,)),
            pltpu.SemaphoreType.DMA((NB,)),
            pltpu.SemaphoreType.DMA((NB,)),
        ],
        compiler_params=pltpu.CompilerParams(
            collective_id=1, has_side_effects=True, vmem_limit_bytes=40 << 20
        ),
        name="bins",
    )(msgs)


def per_device(
    raw_frames, dark_frame, flat_field, pixel_gain, smoothing_kernel, bin_labels, lag_list
):
    tables = [jnp.asarray(a) for a in dft_tables()]
    weighted = ((raw_frames.astype(F32) - dark_frame) * flat_field * pixel_gain).astype(BF16)
    weighted = jnp.transpose(weighted, (1, 0, 2))
    peers = lax.axis_size("rows")
    up = [(i, i + 1) for i in range(peers - 1)]
    down = [(j, i) for i, j in up]
    before = lax.ppermute(weighted[ROWS8 - 2 :], "rows", up)
    after = lax.ppermute(weighted[:2], "rows", down)
    smoothed = smooth(smoothing_kernel, before, weighted, after)
    series = lax.all_to_all(smoothed, "tm", split_axis=2, concat_axis=1, tiled=True)
    lag_rows = jnp.broadcast_to(lag_list[:, None], (LAGS, 128))

    def one_round(step):
        slots, high, low, rounds = slot_tables(step.reshape(1, 1), bin_labels)
        msgs = lag_messages(slots, series, high, low, rounds, lag_rows, tables)
        return bin_sums(msgs)

    sums, most = one_round(jnp.int32(0))
    needed = most[0, 0].astype(jnp.int32)

    def more(state):
        return state[0] < needed

    def again(state):
        step, total = state
        extra, _ = one_round(step)
        return step + 1, total + extra

    _, sums = lax.while_loop(more, again, (jnp.int32(1), sums))
    return sums.reshape(-1)[:HALF]


def solution(mesh):
    return jax.shard_map(
        per_device,
        mesh=mesh,
        in_specs=(
            P("tm", "rows", None),
            P("rows", None),
            P("rows", None),
            P("rows", None),
            P(),
            P("rows", None),
            P(),
        ),
        out_specs=P(("rows", "tm")),
        check_vma=False,
    )
```

```python
import functools

import jax
import jax.numpy as jnp
import numpy as np
from jax import lax
from jax.experimental import pallas as pl
from jax.experimental.pallas import tpu as pltpu
from jax.sharding import PartitionSpec as P

F32 = jnp.float32
BF16 = jnp.bfloat16
MESH = pl.DeviceIdType.MESH
VMEM = pltpu.MemorySpace.VMEM
SMEM = pltpu.MemorySpace.SMEM

ROWS8 = 8
W = 2048
FB = 80
TM = 4
QUARTER = W // TM
FRAMES = FB * TM
LAGS = 64
HALF = 36000
BW = 1152
NB = 64
CAP = 128
NDFT = 400
FPAD = 208
MROWS = 80


def dft_tables():
    t = np.arange(FRAMES)
    f = np.arange(NDFT // 2 + 1)
    angle = 2 * np.pi * ((f[:, None] * t[None, :]) % NDFT) / NDFT
    forward = np.zeros((2 * FPAD, FRAMES), np.float64)
    forward[: f.size] = np.cos(angle)
    forward[FPAD : FPAD + f.size] = np.sin(angle)
    k = np.arange(80)
    back = np.zeros((80, FPAD), np.float64)
    fold = np.full(f.size, 2.0)
    fold[0] = fold[-1] = 1.0
    back[:, : f.size] = np.cos(2 * np.pi * ((k[:, None] * f[None, :]) % NDFT) / NDFT) * fold / NDFT

    def split(a):
        hi = a.astype(jnp.bfloat16)
        lo = (a - hi.astype(np.float64)).astype(jnp.bfloat16)
        return hi, lo

    return (*split(forward), *split(back))


def smooth_row(taps, wp, out, i):
    lane = lax.broadcasted_iota(jnp.int32, (16, 128), 1)
    zero = jnp.zeros((16, 128), F32)
    chunks = W // 128

    def one(fb, carry):
        frames = pl.ds(pl.multiple_of(fb * 16, 16), 16)
        rolled = []

        def finish(c):
            left = rolled[c - 1] if c > 0 else (zero,) * 5
            right = rolled[c + 1] if c + 1 < chunks else (zero,) * 5
            mine = rolled[c]
            total = mine[2]
            total = total + jnp.where(lane >= 2, mine[0], left[0])
            total = total + jnp.where(lane >= 1, mine[1], left[1])
            total = total + jnp.where(lane < 127, mine[3], right[3])
            total = total + jnp.where(lane < 126, mine[4], right[4])
            out[i, frames, c * 128 : (c + 1) * 128] = total.astype(BF16)

        for c in range(chunks):
            rows = [wp[i + a, frames, c * 128 : (c + 1) * 128].astype(F32) for a in range(5)]
            part = []
            for b in range(5):
                acc = rows[0] * taps[0, b]
                for a in range(1, 5):
                    acc = acc + rows[a] * taps[a, b]
                part.append(acc)
            rolled.append(
                (
                    pltpu.roll(part[0], 2, 1),
                    pltpu.roll(part[1], 1, 1),
                    part[2],
                    pltpu.roll(part[3], 127, 1),
                    pltpu.roll(part[4], 126, 1),
                )
            )
            if c >= 1:
                finish(c - 1)
        finish(chunks - 1)
        return carry

    lax.fori_loop(0, FB // 16, one, 0)


def bucket_of(label):
    half = label >= HALF
    inside = jnp.where(half, label - HALF, label)
    quotient = lax.shift_right_logical(lax.shift_right_logical(inside, 7) * 57, 9)
    bucket = jnp.where(half, quotient + 32, quotient)
    return bucket, inside - quotient * BW


def fill_slots(labels, first, slots, parts=None):
    upper = (
        lax.broadcasted_iota(jnp.int32, (QUARTER, QUARTER), 0)
        <= lax.broadcasted_iota(jnp.int32, (QUARTER, QUARTER), 1)
    ).astype(F32).astype(BF16)
    which = lax.broadcasted_iota(jnp.int32, (NB, QUARTER), 0)
    sub = lax.broadcasted_iota(jnp.int32, (8, QUARTER), 0)
    carry = jnp.zeros((NB, 1), F32)
    for i in range(ROWS8):
        bucket, local = bucket_of(labels[i : i + 1, :])
        hot = (which == bucket).astype(F32)
        count = jnp.dot(hot.astype(BF16), upper, preferred_element_type=F32) + carry
        rank = jnp.sum(hot * count, axis=0, keepdims=True).astype(jnp.int32) - 1 - first
        inside = (rank >= 0) & (rank < CAP)
        slots[i : i + 1, :] = jnp.where(inside, bucket * CAP + rank, NB * CAP)
        if parts is not None:
            top = lax.shift_right_logical(local, 7)
            low = local - top * 128
            parts[i] = jnp.where(sub == 0, top.astype(F32), jnp.where(sub == 1, low.astype(F32), 0.0))
        carry = count[:, QUARTER - 1 : QUARTER]
    most = jnp.max(carry, axis=0, keepdims=True)
    return lax.shift_right_logical(most.astype(jnp.int32) + (CAP - 1), 7).astype(F32)


def slot_kernel(step_ref, labels, slots):
    fill_slots(labels, step_ref[0, 0] * CAP, slots)


def later_slots(step, labels):
    return pl.pallas_call(
        slot_kernel,
        out_shape=jax.ShapeDtypeStruct((ROWS8, QUARTER), jnp.int32),
        in_specs=[pl.BlockSpec(memory_space=SMEM), pl.BlockSpec(memory_space=VMEM)],
        out_specs=pl.BlockSpec(memory_space=VMEM),
        name="slots",
    )(step, labels)


def front_kernel(
    taps, raw, dark, flat, gain, all_labels, lag_rows, fhi, flo, bhi, blo,
    src, slots, labels_out,
    wp, smoothed, series, labels, parts,
    hsend, hrecv, zsend, zrecv, lsend, lrecv,
):
    rows = lax.axis_index("rows")
    tm = lax.axis_index("tm")
    over = rows + 4 - 8 * ((rows // 4) % 2)
    not_first = (rows + 31) // 32
    not_last = 1 - (rows + 1) // 32

    barrier = pltpu.get_barrier_semaphore()

    def greet(r, t):
        pl.semaphore_signal(barrier, inc=1, device_id=(r, t), device_id_type=MESH)

    @pl.when(rows > 0)
    def _():
        greet(rows - 1, tm)

    @pl.when(rows < 31)
    def _():
        greet(rows + 1, tm)

    for q in range(TM):
        greet(over, q)

    blocks = FB // 16

    def to_next(q):
        frames = pl.ds(q * 16, 16)
        return pltpu.make_async_remote_copy(
            src_ref=wp.at[8:10, frames], dst_ref=wp.at[0:2, frames],
            send_sem=hsend.at[0, q], recv_sem=hrecv.at[0, q],
            device_id=(rows + 1, tm), device_id_type=MESH,
        )

    def to_previous(q):
        frames = pl.ds(q * 16, 16)
        return pltpu.make_async_remote_copy(
            src_ref=wp.at[2:4, frames], dst_ref=wp.at[10:12, frames],
            send_sem=hsend.at[1, q], recv_sem=hrecv.at[1, q],
            device_id=(rows - 1, tm), device_id_type=MESH,
        )

    label_copy = pltpu.make_async_remote_copy(
        src_ref=all_labels.at[:, pl.ds(pl.multiple_of(tm * QUARTER, QUARTER), QUARTER)],
        dst_ref=labels, send_sem=lsend, recv_sem=lrecv,
        device_id=(over, tm), device_id_type=MESH,
    )

    @pl.when(rows == 0)
    def _():
        wp[0:2] = jnp.zeros((2, FB, W), BF16)

    @pl.when(rows == 31)
    def _():
        wp[10:12] = jnp.zeros((2, FB, W), BF16)

    cols = 256
    for q in range(blocks):

        def weigh(c, carry):
            at = pl.ds(pl.multiple_of(c * cols, cols), cols)
            x = raw[q * 16 : (q + 1) * 16, :, at].astype(F32)
            x = (x - dark[:, at][None]) * flat[:, at][None] * gain[:, at][None]
            wp[2:10, q * 16 : (q + 1) * 16, at] = jnp.swapaxes(x, 0, 1).astype(BF16)
            return carry

        lax.fori_loop(0, W // cols, weigh, 0)

        if q == 0:
            pl.semaphore_wait(barrier, TM + not_first + not_last)
            label_copy.start()

        @pl.when(rows < 31)
        def _():
            to_next(q).start()

        @pl.when(rows > 0)
        def _():
            to_previous(q).start()

    def across(i, q):
        return pltpu.make_async_remote_copy(
            src_ref=smoothed.at[i, :, q * QUARTER : (q + 1) * QUARTER],
            dst_ref=series.at[i, pl.ds(pl.multiple_of(tm * FB, FB), FB), :],
            send_sem=zsend.at[i, q], recv_sem=zrecv.at[i, tm],
            device_id=(over, q), device_id_type=MESH,
        )

    def row(n, carry):
        i = (n + 2) % ROWS8

        @pl.when((n == 4) & (rows < 31))
        def _():
            for q in range(blocks):
                to_previous(q).wait_recv()

        @pl.when((n == 6) & (rows > 0))
        def _():
            for q in range(blocks):
                to_next(q).wait_recv()

        smooth_row(taps, wp, smoothed, i)
        for q in range(TM):
            across(i, q).start()
        return carry

    lax.fori_loop(0, ROWS8, row, 0)

    label_copy.wait_recv()
    labels_out[...] = labels[...]
    rounds = fill_slots(labels, 0, slots, parts)

    lag = lag_rows[...]
    pick = (lag[:, :80] == lax.broadcasted_iota(jnp.int32, (LAGS, 80), 1)).astype(F32).astype(BF16)
    chi = jnp.dot(pick, bhi[...], preferred_element_type=F32).astype(BF16)
    clo = jnp.dot(pick, blo[...], preferred_element_type=F32).astype(BF16)
    scale = 1.0 / (FRAMES - lag[:, :1].astype(F32))
    sub = lax.broadcasted_iota(jnp.int32, (8, QUARTER), 0)

    def lags(n, carry):
        i = (n + 2) % ROWS8
        for t in range(TM):
            pltpu.make_async_copy(
                series.at[i, t * FB : (t + 1) * FB], series.at[i, t * FB : (t + 1) * FB], zrecv.at[i, t]
            ).wait()
        s = series[i]
        x = jnp.dot(fhi[...], s, preferred_element_type=F32)
        x = x + jnp.dot(flo[...], s, preferred_element_type=F32)
        power = x[:FPAD] * x[:FPAD] + x[FPAD:] * x[FPAD:]
        phi = power.astype(BF16)
        plo = (power - phi.astype(F32)).astype(BF16)
        r = jnp.dot(chi, phi, preferred_element_type=F32)
        r = r + jnp.dot(chi, plo, preferred_element_type=F32)
        r = r + jnp.dot(clo, phi, preferred_element_type=F32)
        r = r * scale
        extra = jnp.where(sub == 2, rounds, parts[i])
        full = jnp.concatenate([r, extra, jnp.zeros((56, QUARTER), F32)], axis=0)
        src[pl.ds(pl.multiple_of(i * QUARTER, QUARTER), QUARTER), :] = full.T
        return carry

    lax.fori_loop(0, ROWS8, lags, 0)

    def drain(i, carry):
        for q in range(TM):
            across(i, q).wait_send()
        return carry

    lax.fori_loop(0, ROWS8, drain, 0)
    label_copy.wait_send()
    for q in range(blocks):

        @pl.when(rows < 31)
        def _():
            to_next(q).wait_send()

        @pl.when(rows > 0)
        def _():
            to_previous(q).wait_send()


def frames_to_lags(taps, raw, dark, flat, gain, labels, lag_rows, tables):
    dma = pltpu.SemaphoreType.DMA
    return pl.pallas_call(
        front_kernel,
        out_shape=(
            jax.ShapeDtypeStruct((ROWS8 * QUARTER, 128), F32),
            jax.ShapeDtypeStruct((ROWS8, QUARTER), jnp.int32),
            jax.ShapeDtypeStruct((ROWS8, QUARTER), jnp.int32),
        ),
        in_specs=[pl.BlockSpec(memory_space=SMEM)] + [pl.BlockSpec(memory_space=VMEM)] * 10,
        out_specs=(pl.BlockSpec(memory_space=VMEM),) * 3,
        scratch_shapes=[
            pltpu.VMEM((ROWS8 + 4, FB, W), BF16),
            pltpu.VMEM((ROWS8, FB, W), BF16),
            pltpu.VMEM((ROWS8, FRAMES, QUARTER), BF16),
            pltpu.VMEM((ROWS8, QUARTER), jnp.int32),
            pltpu.VMEM((ROWS8, 8, QUARTER), F32),
            dma((2, FB // 16)),
            dma((2, FB // 16)),
            dma((ROWS8, TM)),
            dma((ROWS8, TM)),
            dma(()),
            dma(()),
        ],
        compiler_params=pltpu.CompilerParams(
            collective_id=0, has_side_effects=True, vmem_limit_bytes=48 << 20
        ),
        name="front",
    )(taps, raw, dark, flat, gain, labels, lag_rows, *tables)


def place_kernel(slots, src, out, dst):
    def clear(j, carry):
        dst[pl.ds(pl.multiple_of(j * 128, 128), 128), :] = jnp.zeros((128, 128), F32)
        return carry

    lax.fori_loop(0, NB, clear, 0)

    per = 16

    def move(g, carry):
        i = g // (QUARTER // per)
        c = (g % (QUARTER // per)) * per
        base = pl.multiple_of(g * per, per)
        for u in range(per):
            to = slots[i, c + u]
            dst[pl.ds(to, 1), :] = src[pl.ds(base + u, 1), :]
        return carry

    lax.fori_loop(0, ROWS8 * QUARTER // per, move, 0)

    def turn(j, carry):
        block = dst[pl.ds(pl.multiple_of(j * 128, 128), 128), :].T
        out[j] = block[:MROWS].astype(BF16)
        return carry

    lax.fori_loop(0, NB, turn, 0)


def place(slots, src):
    return pl.pallas_call(
        place_kernel,
        out_shape=jax.ShapeDtypeStruct((NB, MROWS, CAP), BF16),
        in_specs=[pl.BlockSpec(memory_space=SMEM), pl.BlockSpec(memory_space=VMEM)],
        out_specs=pl.BlockSpec(memory_space=VMEM),
        scratch_shapes=[pltpu.VMEM((NB * CAP + 8, 128), F32)],
        compiler_params=pltpu.CompilerParams(vmem_limit_bytes=40 << 20),
        name="place",
    )(slots, src)


def position():
    rows = lax.axis_index("rows")
    tm = lax.axis_index("tm")
    y = rows // 8
    z = (tm // 2) * 2 + (rows // 4) % 2
    x = rows % 4
    return x, y, z, tm % 2


def at_offset(i, sign):
    x, y, z, _ = position()
    x = (x + sign * (i % 4) + 4) % 4
    y = (y + sign * ((i // 4) % 4) + 4) % 4
    z = (z + sign * (i // 16) + 4) % 4
    rows = y * 8 + (z % 2) * 4 + x
    return rows, z // 2


def bin_kernel(msgs, out, most, recv, acc, tops, fin, got, send_sem, recv_sem, fsend, frecv):
    rows_me = lax.axis_index("rows")
    tm_me = lax.axis_index("tm")
    core = tm_me % 2
    chip = rows_me * 2 + tm_me // 2

    barrier = pltpu.get_barrier_semaphore()

    def greet(i, carry):
        rows, zh = at_offset(i, 1)
        for c in range(2):

            @pl.when((i != 0) | (c != core))
            def _():
                pl.semaphore_signal(barrier, inc=1, device_id=(rows, zh * 2 + c), device_id_type=MESH)

        return carry

    lax.fori_loop(0, NB, greet, 0)
    pl.semaphore_wait(barrier, 2 * NB - 1)

    def route(i, sign):
        rows, zh = at_offset(i, sign)
        there = rows * 2 + zh
        return pltpu.make_async_remote_copy(
            src_ref=msgs.at[there],
            dst_ref=recv.at[i],
            send_sem=send_sem.at[i],
            recv_sem=recv_sem.at[i],
            device_id=(rows, zh * 2 + core),
            device_id_type=MESH,
        )

    def send(i, carry):
        route(i, 1).start()
        return carry

    lax.fori_loop(1, NB, send, 0)

    acc[...] = jnp.zeros_like(acc)
    tops[...] = jnp.zeros_like(tops)
    row_id = lax.broadcasted_iota(jnp.int32, (128, 2 * CAP), 0).astype(F32)

    def add(first, second):
        both = jnp.concatenate([first, second], axis=1)
        values = both[:LAGS]
        extra = both[LAGS : LAGS + 16].astype(F32)
        high, low = extra[0:1], extra[1:2]
        tops[...] = jnp.maximum(tops[...], extra[2:3])
        for h in range(BW // 128):
            key = jnp.where(high == h, low, -1.0)
            hot = jnp.where(row_id == key, 1.0, 0.0).astype(BF16)
            acc[:, h * 128 : (h + 1) * 128] += lax.dot_general(
                values, hot, (((1,), (1,)), ((), ())), preferred_element_type=F32
            )

    route(1, 1).wait_recv()
    add(msgs[chip], recv[1])

    def pair(g, carry):
        i = 2 * g
        route(i, 1).wait_recv()
        route(i + 1, 1).wait_recv()
        add(recv[i], recv[i + 1])
        return carry

    lax.fori_loop(1, NB // 2, pair, 0)

    for h in range(BW // 128):
        fin[:, h, :] = acc[:, h * 128 : (h + 1) * 128]
    peak = jnp.max(tops[...], axis=1, keepdims=True)
    fin[:, BW // 128, :] = jnp.broadcast_to(peak, (LAGS, 128))

    half = chip // 32
    place = core * 32 + chip % 32

    def owner(i):
        rows, zh = at_offset(i, 1)
        there = rows * 2 + zh
        return pltpu.make_async_remote_copy(
            src_ref=fin.at[there],
            dst_ref=got.at[place],
            send_sem=fsend.at[i],
            recv_sem=frecv.at[place],
            device_id=(rows, zh * 2 + half),
            device_id_type=MESH,
        )

    def hand(i, carry):
        owner(i).start()
        return carry

    lax.fori_loop(1, NB, hand, 0)

    own = pltpu.make_async_copy(fin.at[chip], got.at[place], frecv.at[place])

    @pl.when(half == core)
    def _():
        own.start()

    @pl.when(half != core)
    def _():
        owner(0).start()

    def arrived(n, carry):
        pltpu.make_async_copy(got.at[n], got.at[n], frecv.at[n]).wait()
        return carry

    lax.fori_loop(0, NB, arrived, 0)

    top = jnp.zeros((1, 128), F32)
    for j in range(32):
        out[9 * j : 9 * j + 9, :] = got[j, 0:9, :] + got[32 + j, 0:9, :]
        top = jnp.maximum(top, jnp.maximum(got[j, 9:10, :], got[32 + j, 9:10, :]))
    most[...] = jnp.broadcast_to(top, (8, 128))

    def drain(i, carry):
        route(i, 1).wait_send()
        owner(i).wait_send()
        return carry

    lax.fori_loop(1, NB, drain, 0)

    @pl.when(half != core)
    def _():
        owner(0).wait_send()


def bin_sums(msgs):
    return pl.pallas_call(
        bin_kernel,
        out_shape=(
            jax.ShapeDtypeStruct((32 * BW // 128, 128), F32),
            jax.ShapeDtypeStruct((8, 128), F32),
        ),
        in_specs=[pl.BlockSpec(memory_space=VMEM)],
        out_specs=(pl.BlockSpec(memory_space=VMEM),) * 2,
        scratch_shapes=[
            pltpu.VMEM((NB, MROWS, CAP), BF16),
            pltpu.VMEM((LAGS, BW), F32),
            pltpu.VMEM((1, 2 * CAP), F32),
            pltpu.VMEM((LAGS, BW // 128 + 1, 128), F32),
            pltpu.VMEM((NB, BW // 128 + 1, 128), F32),
            pltpu.SemaphoreType.DMA((NB,)),
            pltpu.SemaphoreType.DMA((NB,)),
            pltpu.SemaphoreType.DMA((NB,)),
            pltpu.SemaphoreType.DMA((NB,)),
        ],
        compiler_params=pltpu.CompilerParams(
            collective_id=1, has_side_effects=True, vmem_limit_bytes=40 << 20
        ),
        name="bins",
    )(msgs)


def per_device(
    raw_frames, dark_frame, flat_field, pixel_gain, smoothing_kernel, bin_labels, lag_list
):
    tables = [jnp.asarray(a) for a in dft_tables()]
    lag_rows = jnp.broadcast_to(lag_list[:, None], (LAGS, 128))
    src, slots, labels = frames_to_lags(
        smoothing_kernel, raw_frames, dark_frame, flat_field, pixel_gain, bin_labels, lag_rows, tables
    )
    sums, most = bin_sums(place(slots, src))
    needed = most[0, 0].astype(jnp.int32)

    def more(state):
        return state[0] < needed

    def again(state):
        step, total = state
        extra, _ = bin_sums(place(later_slots(step.reshape(1, 1), labels), src))
        return step + 1, total + extra

    _, sums = lax.while_loop(more, again, (jnp.int32(1), sums))
    return sums.reshape(-1)[:HALF]


def solution(mesh):
    return jax.shard_map(
        per_device,
        mesh=mesh,
        in_specs=(
            P("tm", "rows", None),
            P("rows", None),
            P("rows", None),
            P("rows", None),
            P(),
            P("rows", None),
            P(),
        ),
        out_specs=P(("rows", "tm")),
        check_vma=False,
    )
```

```python
import functools

import jax
import jax.numpy as jnp
import numpy as np
from jax import lax
from jax.experimental import pallas as pl
from jax.experimental.pallas import tpu as pltpu
from jax.sharding import PartitionSpec as P

F32 = jnp.float32
BF16 = jnp.bfloat16
MESH = pl.DeviceIdType.MESH
VMEM = pltpu.MemorySpace.VMEM
SMEM = pltpu.MemorySpace.SMEM

ROWS8 = 8
W = 2048
FB = 80
TM = 4
QUARTER = W // TM
FRAMES = FB * TM
LAGS = 64
HALF = 36000
BW = 1152
NB = 64
CAP = 128
NDFT = 400
FPAD = 208
MROWS = 80


def dft_tables():
    t = np.arange(FRAMES)
    f = np.arange(NDFT // 2 + 1)
    angle = 2 * np.pi * ((f[:, None] * t[None, :]) % NDFT) / NDFT
    forward = np.zeros((2 * FPAD, FRAMES), np.float64)
    forward[: f.size] = np.cos(angle)
    forward[FPAD : FPAD + f.size] = np.sin(angle)
    k = np.arange(80)
    back = np.zeros((80, FPAD), np.float64)
    fold = np.full(f.size, 2.0)
    fold[0] = fold[-1] = 1.0
    back[:, : f.size] = np.cos(2 * np.pi * ((k[:, None] * f[None, :]) % NDFT) / NDFT) * fold / NDFT

    def split(a):
        hi = a.astype(jnp.bfloat16)
        lo = (a - hi.astype(np.float64)).astype(jnp.bfloat16)
        return hi, lo

    return (*split(forward), *split(back))


def position():
    rows = lax.axis_index("rows")
    tm = lax.axis_index("tm")
    return rows % 4, rows // 8, (tm // 2) * 2 + (rows // 4) % 2, tm % 2


def device(x, y, z, core):
    return (y * 8 + (z % 2) * 4 + x, (z // 2) * 2 + core)


def at_offset(i):
    x, y, z, _ = position()
    i = (i * 37) % NB
    rows, tm = device((x + i % 4) % 4, (y + (i // 4) % 4) % 4, (z + i // 16) % 4, 0)
    return rows, tm // 2


def signal(sem, where):
    pl.semaphore_signal(sem, inc=1, device_id=where, device_id_type=MESH)


def spread_partner(k):
    x, y, z, core = position()
    return (
        lambda: device(x, y, z, 1 - core),
        lambda: device((x + 1) % 4, y, z, core),
        lambda: device((x + 2) % 4, y, z, core),
        lambda: device(x, (y + 1) % 4, z, core),
        lambda: device(x, (y + 2) % 4, z, core),
        lambda: device(x, y, (z + 1) % 4, core),
        lambda: device(x, y, (z + 2) % 4, core),
    )[k]()


SPREAD = 7


def spread_round(k, sems):
    if k > 0:
        pl.semaphore_wait(sems.at[k - 1], 1)
    if k < SPREAD:
        signal(sems.at[k], spread_partner(k))


def greet_near(barrier):
    x, y, z, core = position()
    for where in (
        device(x, y, z, 1 - core),
        device((x + 1) % 4, y, z, core),
        device((x + 3) % 4, y, z, core),
        device((x + 2) % 4, y, z, core),
        device(x, (y + 1) % 4, z, core),
        device(x, (y + 3) % 4, z, core),
        device(x, (y + 2) % 4, z, core),
        device(x, y, (z + 2) % 4, core),
    ):
        signal(barrier, where)
    return 8


def smooth_block(taps, wp, out, i, fb):
    lane = lax.broadcasted_iota(jnp.int32, (16, 128), 1)
    zero = jnp.zeros((16, 128), F32)
    chunks = W // 128
    frames = pl.ds(pl.multiple_of(fb * 16, 16), 16)
    rolled = []

    def finish(c):
        left = rolled[c - 1] if c > 0 else (zero,) * 5
        right = rolled[c + 1] if c + 1 < chunks else (zero,) * 5
        mine = rolled[c]
        total = mine[2]
        total = total + jnp.where(lane >= 2, mine[0], left[0])
        total = total + jnp.where(lane >= 1, mine[1], left[1])
        total = total + jnp.where(lane < 127, mine[3], right[3])
        total = total + jnp.where(lane < 126, mine[4], right[4])
        out[i, frames, c * 128 : (c + 1) * 128] = total.astype(BF16)

    for c in range(chunks):
        rows = [wp[i + a, frames, c * 128 : (c + 1) * 128].astype(F32) for a in range(5)]
        part = []
        for b in range(5):
            acc = rows[0] * taps[0, b]
            for a in range(1, 5):
                acc = acc + rows[a] * taps[a, b]
            part.append(acc)
        rolled.append(
            (
                pltpu.roll(part[0], 2, 1),
                pltpu.roll(part[1], 1, 1),
                part[2],
                pltpu.roll(part[3], 127, 1),
                pltpu.roll(part[4], 126, 1),
            )
        )
        if c >= 1:
            finish(c - 1)
    finish(chunks - 1)


def bucket_of(label):
    half = label >= HALF
    inside = jnp.where(half, label - HALF, label)
    quotient = lax.shift_right_logical(lax.shift_right_logical(inside, 7) * 57, 9)
    bucket = jnp.where(half, quotient + 32, quotient)
    return bucket, inside - quotient * BW


def fill_slots(labels, first, buckets, ranks, parts=None):
    upper = (
        lax.broadcasted_iota(jnp.int32, (QUARTER, QUARTER), 0)
        <= lax.broadcasted_iota(jnp.int32, (QUARTER, QUARTER), 1)
    ).astype(F32).astype(BF16)
    which = lax.broadcasted_iota(jnp.int32, (NB, QUARTER), 0)
    sub = lax.broadcasted_iota(jnp.int32, (8, QUARTER), 0)
    carry = jnp.zeros((NB, 1), F32)
    for i in range(ROWS8):
        bucket, local = bucket_of(labels[i : i + 1, :])
        hot = (which == bucket).astype(F32)
        count = jnp.dot(hot.astype(BF16), upper, preferred_element_type=F32) + carry
        rank = jnp.sum(hot * count, axis=0, keepdims=True) - 1.0 - first
        ranks[i : i + 1, :] = jnp.where((rank >= 0) & (rank < CAP), rank, -1024.0)
        buckets[i : i + 1, :] = bucket.astype(F32)
        if parts is not None:
            top = lax.shift_right_logical(local, 7)
            low = local - top * 128
            parts[i] = jnp.where(sub == 0, top.astype(F32), jnp.where(sub == 1, low.astype(F32), 0.0))
        carry = count[:, QUARTER - 1 : QUARTER]
    most = jnp.max(carry, axis=0, keepdims=True)
    return lax.shift_right_logical(most.astype(jnp.int32) + (CAP - 1), 7).astype(F32)


def route_and_bin(values, buckets, ranks, out, most, msgs, recv, acc, tops, fin, got, sems):
    send_sem, recv_sem, fsend, frecv, own_sem = sems
    rows_me = lax.axis_index("rows")
    tm_me = lax.axis_index("tm")
    core = tm_me % 2
    chip = rows_me * 2 + tm_me // 2

    def route(i):
        rows, zh = at_offset(i)
        return pltpu.make_async_remote_copy(
            src_ref=msgs.at[i],
            dst_ref=recv.at[i],
            send_sem=send_sem.at[i],
            recv_sem=recv_sem.at[i],
            device_id=(rows, zh * 2 + core),
            device_id_type=MESH,
        )

    def chip_at(i):
        rows, zh = at_offset(i)
        return (rows * 2 + zh).astype(F32)

    slot_id = lax.broadcasted_iota(jnp.int32, (2 * CAP, QUARTER), 0).astype(F32)

    def fill(g):
        first, second = chip_at(2 * g), chip_at(2 * g + 1)
        b = buckets[...]
        r = ranks[...]
        key = jnp.where(b == first, r, jnp.where(b == second, r + CAP, -1.0))
        total = jnp.zeros((MROWS, 2 * CAP), F32)
        for i in range(ROWS8):
            hot = jnp.where(slot_id == key[i : i + 1, :], 1.0, 0.0).astype(BF16)
            total = total + lax.dot_general(
                values[i], hot, (((1,), (1,)), ((), ())), preferred_element_type=F32
            )
        return total.astype(BF16)

    both = fill(0)
    recv[0] = both[:, :CAP]
    msgs[1] = both[:, CAP:]
    route(1).start()

    def send(g, carry):
        both = fill(g)
        msgs[2 * g] = both[:, :CAP]
        msgs[2 * g + 1] = both[:, CAP:]
        route(2 * g).start()
        route(2 * g + 1).start()
        return carry

    lax.fori_loop(1, NB // 2, send, 0)

    acc[...] = jnp.zeros_like(acc)
    tops[...] = jnp.zeros_like(tops)
    row_id = lax.broadcasted_iota(jnp.int32, (128, 2 * CAP), 0).astype(F32)

    def add(first, second):
        both = jnp.concatenate([first, second], axis=1)
        extra = both[LAGS : LAGS + 16].astype(F32)
        high, low = extra[0:1], extra[1:2]
        tops[...] = jnp.maximum(tops[...], extra[2:3])
        for h in range(BW // 128):
            key = jnp.where(high == h, low, -1.0)
            hot = jnp.where(row_id == key, 1.0, 0.0).astype(BF16)
            acc[:, h * 128 : (h + 1) * 128] += lax.dot_general(
                both[:LAGS], hot, (((1,), (1,)), ((), ())), preferred_element_type=F32
            )

    route(1).wait_recv()
    add(recv[0], recv[1])

    def pair(g, carry):
        i = 2 * g
        route(i).wait_recv()
        route(i + 1).wait_recv()
        add(recv[i], recv[i + 1])
        return carry

    lax.fori_loop(1, NB // 2, pair, 0)

    for h in range(BW // 128):
        fin[:, h, :] = acc[:, h * 128 : (h + 1) * 128]
    peak = jnp.max(tops[...], axis=1, keepdims=True)
    fin[:, BW // 128, :] = jnp.broadcast_to(peak, (LAGS, 128))

    half = chip // 32
    spot = core * 32 + chip % 32

    def owner(i):
        rows, zh = at_offset(i)
        return pltpu.make_async_remote_copy(
            src_ref=fin.at[rows * 2 + zh],
            dst_ref=got.at[spot],
            send_sem=fsend.at[i],
            recv_sem=frecv.at[spot],
            device_id=(rows, zh * 2 + half),
            device_id_type=MESH,
        )

    def hand(i, carry):
        owner(i).start()
        return carry

    lax.fori_loop(1, NB, hand, 0)

    own = pltpu.make_async_copy(fin.at[chip], got.at[spot], frecv.at[spot])

    @pl.when(half == core)
    def _():
        own.start()

    @pl.when(half != core)
    def _():
        owner(0).start()

    def arrived(n, carry):
        pltpu.make_async_copy(got.at[n], got.at[n], frecv.at[n]).wait()
        return carry

    lax.fori_loop(0, NB, arrived, 0)

    top = jnp.zeros((1, 128), F32)
    for j in range(32):
        out[9 * j : 9 * j + 9, :] = got[j, 0:9, :] + got[32 + j, 0:9, :]
        top = jnp.maximum(top, jnp.maximum(got[j, 9:10, :], got[32 + j, 9:10, :]))
    most[...] = jnp.broadcast_to(top, (8, 128))

    def drain(i, carry):
        route(i).wait_send()
        owner(i).wait_send()
        return carry

    lax.fori_loop(1, NB, drain, 0)

    @pl.when(half != core)
    def _():
        owner(0).wait_send()


def route_scratch():
    dma = pltpu.SemaphoreType.DMA
    return [
        pltpu.VMEM((NB, MROWS, CAP), BF16),
        pltpu.VMEM((NB, MROWS, CAP), BF16),
        pltpu.VMEM((LAGS, BW), F32),
        pltpu.VMEM((1, 2 * CAP), F32),
        pltpu.VMEM((LAGS, BW // 128 + 1, 128), F32),
        pltpu.VMEM((NB, BW // 128 + 1, 128), F32),
        dma((NB,)),
        dma((NB,)),
        dma((NB,)),
        dma((NB,)),
        dma(()),
    ]


SUMS = (
    jax.ShapeDtypeStruct((32 * BW // 128, 128), F32),
    jax.ShapeDtypeStruct((8, 128), F32),
)


def again_kernel(step_ref, values, labels, out, most, buckets, ranks, spread, *scratch):
    barrier = pltpu.get_barrier_semaphore()
    near = greet_near(barrier)
    x, y, z, core = position()
    signal(barrier, device(x, y, (z + 1) % 4, core))
    signal(barrier, device(x, y, (z + 3) % 4, core))
    pl.semaphore_wait(barrier, near + 2)
    for k in range(SPREAD + 1):
        spread_round(k, spread)
    fill_slots(labels, (step_ref[0, 0] * CAP).astype(F32), buckets, ranks)
    route_and_bin(values, buckets, ranks, out, most, *scratch[:6], scratch[6:])


def another_round(step, values, labels):
    return pl.pallas_call(
        again_kernel,
        out_shape=SUMS,
        in_specs=[
            pl.BlockSpec(memory_space=SMEM),
            pl.BlockSpec(memory_space=VMEM),
            pl.BlockSpec(memory_space=VMEM),
        ],
        out_specs=(pl.BlockSpec(memory_space=VMEM),) * 2,
        scratch_shapes=[
            pltpu.VMEM((ROWS8, QUARTER), F32),
            pltpu.VMEM((ROWS8, QUARTER), F32),
            pltpu.SemaphoreType.REGULAR((SPREAD,)),
            *route_scratch(),
        ],
        compiler_params=pltpu.CompilerParams(
            collective_id=1, has_side_effects=True, vmem_limit_bytes=40 << 20
        ),
        name="again",
    )(step, values, labels)


def main_kernel(
    taps, raw_in, dark_in, flat_in, gain_in, labels_in, lag_in, fhi_in, flo_in, bhi_in, blo_in,
    out, most, values_out, labels_out,
    raw, dark, flat, gain, all_labels, lag_row, fhi, flo, bhi, blo, in_sem,
    wp, smoothed, series, labels, parts, values, buckets, ranks,
    hsend, hrecv, msend, mrecv, esend, erecv, lsend, lrecv, spread, keep_sem, *scratch,
):
    rows = lax.axis_index("rows")
    tm = lax.axis_index("tm")
    over = rows + 4 - 8 * ((rows // 4) % 2)
    not_first = (rows + 31) // 32
    not_last = 1 - (rows + 1) // 32
    blocks = FB // 16

    ins = [pltpu.make_async_copy(a, b, in_sem.at[n]) for n, (a, b) in enumerate((
        (dark_in, dark), (flat_in, flat), (gain_in, gain), (labels_in, all_labels),
        (lag_in, lag_row), (fhi_in, fhi), (flo_in, flo), (bhi_in, bhi), (blo_in, blo),
    ))]
    raws = [
        pltpu.make_async_copy(raw_in.at[pl.ds(q * 16, 16)], raw.at[pl.ds(q * 16, 16)], in_sem.at[9 + q])
        for q in range(blocks)
    ]
    for copy in ins[:3]:
        copy.start()
    for copy in raws:
        copy.start()
    for copy in ins[3:]:
        copy.start()

    barrier = pltpu.get_barrier_semaphore()

    @pl.when(rows > 0)
    def _():
        signal(barrier, (rows - 1, tm))

    @pl.when(rows < 31)
    def _():
        signal(barrier, (rows + 1, tm))

    for q in range(TM):
        signal(barrier, (over, q))
    near = greet_near(barrier)

    def to_next(q):
        frames = pl.ds(pl.multiple_of(q * 16, 16), 16)
        return pltpu.make_async_remote_copy(
            src_ref=wp.at[8:10, frames], dst_ref=wp.at[0:2, frames],
            send_sem=hsend.at[0, q], recv_sem=hrecv.at[0, q],
            device_id=(rows + 1, tm), device_id_type=MESH,
        )

    def to_previous(q):
        frames = pl.ds(pl.multiple_of(q * 16, 16), 16)
        return pltpu.make_async_remote_copy(
            src_ref=wp.at[2:4, frames], dst_ref=wp.at[10:12, frames],
            send_sem=hsend.at[1, q], recv_sem=hrecv.at[1, q],
            device_id=(rows - 1, tm), device_id_type=MESH,
        )

    label_copy = pltpu.make_async_remote_copy(
        src_ref=all_labels.at[:, pl.ds(pl.multiple_of(tm * QUARTER, QUARTER), QUARTER)],
        dst_ref=labels, send_sem=lsend, recv_sem=lrecv,
        device_id=(over, tm), device_id_type=MESH,
    )

    @pl.when(rows == 0)
    def _():
        wp[0:2] = jnp.zeros((2, FB, W), BF16)

    @pl.when(rows == 31)
    def _():
        wp[10:12] = jnp.zeros((2, FB, W), BF16)

    for copy in ins[:3]:
        copy.wait()
    cols = 256
    for q in range(blocks):
        raws[q].wait()

        def weigh(c, carry):
            at = pl.ds(pl.multiple_of(c * cols, cols), cols)
            v = raw[q * 16 : (q + 1) * 16, :, at].astype(F32)
            v = (v - dark[:, at][None]) * flat[:, at][None] * gain[:, at][None]
            wp[2:10, q * 16 : (q + 1) * 16, at] = jnp.swapaxes(v, 0, 1).astype(BF16)
            return carry

        lax.fori_loop(0, W // cols, weigh, 0)

        if q == 0:
            pl.semaphore_wait(barrier, near + TM + not_first + not_last)

        @pl.when(rows < 31)
        def _():
            to_next(q).start()

        @pl.when(rows > 0)
        def _():
            to_previous(q).start()

    ins[3].wait()
    label_copy.start()

    def mine(t):
        return pl.ds(pl.multiple_of(t * FB, FB), FB)

    def across(i, q):
        return pltpu.make_async_remote_copy(
            src_ref=smoothed.at[i, :, q * QUARTER : (q + 1) * QUARTER],
            dst_ref=series.at[i, mine(tm), :],
            send_sem=msend.at[i, q], recv_sem=mrecv.at[i, tm],
            device_id=(over, q), device_id_type=MESH,
        )

    def across_edge(e, fb, q):
        return pltpu.make_async_remote_copy(
            src_ref=smoothed.at[
                pl.ds(6 * e, 2), pl.ds(pl.multiple_of(fb * 16, 16), 16), q * QUARTER : (q + 1) * QUARTER
            ],
            dst_ref=series.at[pl.ds(6 * e, 2), pl.ds(pl.multiple_of(tm * FB + fb * 16, 16), 16), :],
            send_sem=esend.at[e, fb, q], recv_sem=erecv.at[e, fb, tm],
            device_id=(over, q), device_id_type=MESH,
        )

    def middle(i, carry):
        for k in range(4):

            @pl.when(i == k + 2)
            def _():
                spread_round(k, spread)

        def one(fb, c):
            smooth_block(taps, wp, smoothed, i, fb)
            return c

        lax.fori_loop(0, blocks, one, 0)
        for q in range(TM):
            across(i, q).start()
        return carry

    lax.fori_loop(2, 6, middle, 0)

    def edges(n, carry):
        fb = n // 2
        e = n % 2
        for k in range(4, SPREAD + 1):

            @pl.when(n == 2 * (k - 4))
            def _():
                spread_round(k, spread)

        @pl.when((e == 0) & (rows > 0))
        def _():
            to_next(fb).wait_recv()

        @pl.when((e == 1) & (rows < 31))
        def _():
            to_previous(fb).wait_recv()

        def one(j, c):
            smooth_block(taps, wp, smoothed, 6 * e + j, fb)
            return c

        lax.fori_loop(0, 2, one, 0)
        for q in range(TM):
            across_edge(e, fb, q).start()
        return carry

    lax.fori_loop(0, 2 * blocks, edges, 0)

    label_copy.wait_recv()
    keep_labels = pltpu.make_async_copy(labels, labels_out, keep_sem.at[0])
    keep_labels.start()
    rounds = fill_slots(labels, 0.0, buckets, ranks, parts)

    for copy in ins[4:]:
        copy.wait()
    turned = (
        lax.broadcasted_iota(jnp.int32, (128, LAGS), 0) == lag_row[...]
    ).astype(F32).T
    pick = turned[:, :80].astype(BF16)
    lag = jnp.sum(
        turned * lax.broadcasted_iota(jnp.int32, (LAGS, 128), 1).astype(F32), axis=1, keepdims=True
    )
    chi = jnp.dot(pick, bhi[...], preferred_element_type=F32).astype(BF16)
    clo = jnp.dot(pick, blo[...], preferred_element_type=F32).astype(BF16)
    scale = 1.0 / (FRAMES - lag)
    sub = lax.broadcasted_iota(jnp.int32, (8, QUARTER), 0)

    def lags(i, carry):
        s = series[i]
        x = jnp.dot(fhi[...], s, preferred_element_type=F32)
        x = x + jnp.dot(flo[...], s, preferred_element_type=F32)
        power = x[:FPAD] * x[:FPAD] + x[FPAD:] * x[FPAD:]
        phi = power.astype(BF16)
        plo = (power - phi.astype(F32)).astype(BF16)
        r = jnp.dot(chi, phi, preferred_element_type=F32)
        r = r + jnp.dot(chi, plo, preferred_element_type=F32)
        r = r + jnp.dot(clo, phi, preferred_element_type=F32)
        r = r * scale
        extra = jnp.where(sub == 2, rounds, parts[i])
        full = jnp.concatenate([r, extra, jnp.zeros((MROWS - LAGS - 8, QUARTER), F32)], axis=0)
        values[i] = full.astype(BF16)
        return carry

    def middle_lags(i, carry):
        for t in range(TM):
            part = series.at[i, pl.ds(t * FB, FB)]
            pltpu.make_async_copy(part, part, mrecv.at[i, t]).wait()
        return lags(i, carry)

    lax.fori_loop(2, 6, middle_lags, 0)

    def edge_lags(e, carry):
        for t in range(TM):
            for fb in range(blocks):
                part = series.at[pl.ds(6 * e, 2), pl.ds(t * FB + fb * 16, 16)]
                pltpu.make_async_copy(part, part, erecv.at[e, fb, t]).wait()
        lags(6 * e, carry)
        return lags(6 * e + 1, carry)

    lax.fori_loop(0, 2, edge_lags, 0)
    keep_values = pltpu.make_async_copy(values, values_out, keep_sem.at[1])
    keep_values.start()

    route_and_bin(values, buckets, ranks, out, most, *scratch[:6], scratch[6:])

    def drain(i, carry):
        for q in range(TM):
            across(i, q).wait_send()
        return carry

    lax.fori_loop(2, 6, drain, 0)

    def drain_edges(n, carry):
        for q in range(TM):
            across_edge(n % 2, n // 2, q).wait_send()
        return carry

    lax.fori_loop(0, 2 * blocks, drain_edges, 0)
    label_copy.wait_send()
    for q in range(blocks):

        @pl.when(rows < 31)
        def _():
            to_next(q).wait_send()

        @pl.when(rows > 0)
        def _():
            to_previous(q).wait_send()

    keep_labels.wait()
    keep_values.wait()


def first_round(taps, raw, dark, flat, gain, labels, lag_row, tables):
    dma = pltpu.SemaphoreType.DMA
    hbm = pl.BlockSpec(memory_space=pltpu.MemorySpace.HBM)
    vmem = pl.BlockSpec(memory_space=VMEM)
    blocks = FB // 16
    plane = (ROWS8, W)
    return pl.pallas_call(
        main_kernel,
        out_shape=(
            *SUMS,
            jax.ShapeDtypeStruct((ROWS8, MROWS, QUARTER), BF16),
            jax.ShapeDtypeStruct((ROWS8, QUARTER), jnp.int32),
        ),
        in_specs=[pl.BlockSpec(memory_space=SMEM)] + [hbm] * 10,
        out_specs=(vmem, vmem, hbm, hbm),
        scratch_shapes=[
            pltpu.VMEM((FB, ROWS8, W), BF16),
            pltpu.VMEM(plane, F32),
            pltpu.VMEM(plane, F32),
            pltpu.VMEM(plane, F32),
            pltpu.VMEM(plane, jnp.int32),
            pltpu.VMEM((1, LAGS), jnp.int32),
            pltpu.VMEM((2 * FPAD, FRAMES), BF16),
            pltpu.VMEM((2 * FPAD, FRAMES), BF16),
            pltpu.VMEM((80, FPAD), BF16),
            pltpu.VMEM((80, FPAD), BF16),
            dma((9 + blocks,)),
            pltpu.VMEM((ROWS8 + 4, FB, W), BF16),
            pltpu.VMEM((ROWS8, FB, W), BF16),
            pltpu.VMEM((ROWS8, FRAMES, QUARTER), BF16),
            pltpu.VMEM((ROWS8, QUARTER), jnp.int32),
            pltpu.VMEM((ROWS8, 8, QUARTER), F32),
            pltpu.VMEM((ROWS8, MROWS, QUARTER), BF16),
            pltpu.VMEM((ROWS8, QUARTER), F32),
            pltpu.VMEM((ROWS8, QUARTER), F32),
            dma((2, blocks)),
            dma((2, blocks)),
            dma((ROWS8, TM)),
            dma((ROWS8, TM)),
            dma((2, blocks, TM)),
            dma((2, blocks, TM)),
            dma(()),
            dma(()),
            pltpu.SemaphoreType.REGULAR((SPREAD,)),
            dma((2,)),
            *route_scratch(),
        ],
        compiler_params=pltpu.CompilerParams(
            collective_id=0, has_side_effects=True, vmem_limit_bytes=56 << 20
        ),
        name="first",
    )(taps, raw, dark, flat, gain, labels, lag_row, *tables)


def per_device(
    raw_frames, dark_frame, flat_field, pixel_gain, smoothing_kernel, bin_labels, lag_list
):
    tables = [jnp.asarray(a) for a in dft_tables()]
    sums, most, values, labels = first_round(
        smoothing_kernel, raw_frames, dark_frame, flat_field, pixel_gain, bin_labels,
        lag_list.reshape(1, LAGS), tables,
    )
    needed = most[0, 0].astype(jnp.int32)

    def more(state):
        return state[0] < needed

    def again(state):
        step, total = state
        extra, _ = another_round(step.reshape(1, 1), values, labels)
        return step + 1, total + extra

    _, sums = lax.while_loop(more, again, (jnp.int32(1), sums))
    return sums.reshape(-1)[:HALF]


def solution(mesh):
    return jax.shard_map(
        per_device,
        mesh=mesh,
        in_specs=(
            P("tm", "rows", None),
            P("rows", None),
            P("rows", None),
            P("rows", None),
            P(),
            P("rows", None),
            P(),
        ),
        out_specs=P(("rows", "tm")),
        check_vma=False,
    )
```

```python
import functools

import jax
import jax.numpy as jnp
import numpy as np
from jax import lax
from jax.experimental import pallas as pl
from jax.experimental.pallas import tpu as pltpu
from jax.sharding import PartitionSpec as P

F32 = jnp.float32
BF16 = jnp.bfloat16
MESH = pl.DeviceIdType.MESH
VMEM = pltpu.MemorySpace.VMEM
SMEM = pltpu.MemorySpace.SMEM

ROWS8 = 8
W = 2048
FB = 80
TM = 4
QUARTER = W // TM
FRAMES = FB * TM
LAGS = 64
HALF = 36000
BW = 1152
NB = 64
CAP = 128
NDFT = 400
FPAD = 208
MROWS = 72


def dft_tables():
    t = np.arange(FRAMES)
    f = np.arange(NDFT // 2 + 1)
    angle = 2 * np.pi * ((f[:, None] * t[None, :]) % NDFT) / NDFT
    forward = np.zeros((2 * FPAD, FRAMES), np.float64)
    forward[: f.size] = np.cos(angle)
    forward[FPAD : FPAD + f.size] = np.sin(angle)
    k = np.arange(80)
    back = np.zeros((80, FPAD), np.float64)
    fold = np.full(f.size, 2.0)
    fold[0] = fold[-1] = 1.0
    back[:, : f.size] = np.cos(2 * np.pi * ((k[:, None] * f[None, :]) % NDFT) / NDFT) * fold / NDFT

    def split(a):
        hi = a.astype(jnp.bfloat16)
        lo = (a - hi.astype(np.float64)).astype(jnp.bfloat16)
        return hi, lo

    return (*split(forward), *split(back))


def position():
    rows = lax.axis_index("rows")
    tm = lax.axis_index("tm")
    return rows % 4, rows // 8, (tm // 2) * 2 + (rows // 4) % 2, tm % 2


def device(x, y, z, core):
    return (y * 8 + (z % 2) * 4 + x, (z // 2) * 2 + core)


def at_offset(i):
    x, y, z, _ = position()
    i = (i * 37) % NB
    rows, tm = device((x + i % 4) % 4, (y + (i // 4) % 4) % 4, (z + i // 16) % 4, 0)
    return rows, tm // 2


def signal(sem, where):
    pl.semaphore_signal(sem, inc=1, device_id=where, device_id_type=MESH)


def spread_partner(k):
    x, y, z, core = position()
    return (
        lambda: device(x, y, z, 1 - core),
        lambda: device((x + 1) % 4, y, z, core),
        lambda: device((x + 2) % 4, y, z, core),
        lambda: device(x, (y + 1) % 4, z, core),
        lambda: device(x, (y + 2) % 4, z, core),
        lambda: device(x, y, (z + 1) % 4, core),
        lambda: device(x, y, (z + 2) % 4, core),
    )[k]()


SPREAD = 7


def spread_round(k, sems):
    if k > 0:
        pl.semaphore_wait(sems.at[k - 1], 1)
    if k < SPREAD:
        signal(sems.at[k], spread_partner(k))


def greet_near(barrier):
    x, y, z, core = position()
    for where in (
        device(x, y, z, 1 - core),
        device((x + 1) % 4, y, z, core),
        device((x + 3) % 4, y, z, core),
        device((x + 2) % 4, y, z, core),
        device(x, (y + 1) % 4, z, core),
        device(x, (y + 3) % 4, z, core),
        device(x, (y + 2) % 4, z, core),
        device(x, y, (z + 2) % 4, core),
    ):
        signal(barrier, where)
    return 8


def smooth_block(taps, wp, out, i, fb):
    lane = lax.broadcasted_iota(jnp.int32, (16, 128), 1)
    zero = jnp.zeros((16, 128), F32)
    chunks = W // 128
    frames = pl.ds(pl.multiple_of(fb * 16, 16), 16)
    rolled = []

    def finish(c):
        left = rolled[c - 1] if c > 0 else (zero,) * 5
        right = rolled[c + 1] if c + 1 < chunks else (zero,) * 5
        mine = rolled[c]
        total = mine[2]
        total = total + jnp.where(lane >= 2, mine[0], left[0])
        total = total + jnp.where(lane >= 1, mine[1], left[1])
        total = total + jnp.where(lane < 127, mine[3], right[3])
        total = total + jnp.where(lane < 126, mine[4], right[4])
        out[i, frames, c * 128 : (c + 1) * 128] = total.astype(BF16)

    for c in range(chunks):
        rows = [wp[i + a, frames, c * 128 : (c + 1) * 128].astype(F32) for a in range(5)]
        part = []
        for b in range(5):
            acc = rows[0] * taps[0, b]
            for a in range(1, 5):
                acc = acc + rows[a] * taps[a, b]
            part.append(acc)
        rolled.append(
            (
                pltpu.roll(part[0], 2, 1),
                pltpu.roll(part[1], 1, 1),
                part[2],
                pltpu.roll(part[3], 127, 1),
                pltpu.roll(part[4], 126, 1),
            )
        )
        if c >= 1:
            finish(c - 1)
    finish(chunks - 1)


def bucket_of(label):
    half = label >= HALF
    inside = jnp.where(half, label - HALF, label)
    quotient = lax.shift_right_logical(lax.shift_right_logical(inside, 7) * 57, 9)
    bucket = jnp.where(half, quotient + 32, quotient)
    return bucket, inside - quotient * BW


def fill_slots(labels, first, buckets, ranks, parts=None):
    upper = (
        lax.broadcasted_iota(jnp.int32, (QUARTER, QUARTER), 0)
        <= lax.broadcasted_iota(jnp.int32, (QUARTER, QUARTER), 1)
    ).astype(F32).astype(BF16)
    which = lax.broadcasted_iota(jnp.int32, (NB, QUARTER), 0)
    sub = lax.broadcasted_iota(jnp.int32, (8, QUARTER), 0)
    carry = jnp.zeros((NB, 1), F32)
    for i in range(ROWS8):
        bucket, local = bucket_of(labels[i : i + 1, :])
        hot = (which == bucket).astype(F32)
        count = jnp.dot(hot.astype(BF16), upper, preferred_element_type=F32) + carry
        rank = jnp.sum(hot * count, axis=0, keepdims=True) - 1.0 - first
        ranks[i : i + 1, :] = jnp.where((rank >= 0) & (rank < CAP), rank, -1024.0)
        buckets[i : i + 1, :] = bucket.astype(F32)
        if parts is not None:
            top = lax.shift_right_logical(local, 7)
            low = local - top * 128
            parts[i] = jnp.where(sub == 0, top.astype(F32), jnp.where(sub == 1, low.astype(F32), 0.0))
        carry = count[:, QUARTER - 1 : QUARTER]
    most = jnp.max(carry, axis=0, keepdims=True)
    return lax.shift_right_logical(most.astype(jnp.int32) + (CAP - 1), 7).astype(F32)


def chip_at(i):
    rows, zh = at_offset(i)
    return (rows * 2 + zh).astype(F32)


def in_slots(g, rows, values, buckets, ranks):
    slot_id = lax.broadcasted_iota(jnp.int32, (2 * CAP, QUARTER), 0).astype(F32)
    b = buckets[...]
    r = ranks[...]
    key = jnp.where(b == chip_at(2 * g), r, jnp.where(b == chip_at(2 * g + 1), r + CAP, -1.0))
    total = jnp.zeros((MROWS, 2 * CAP), F32)
    for i in rows:
        hot = jnp.where(slot_id == key[i : i + 1, :], 1.0, 0.0).astype(BF16)
        total = total + lax.dot_general(
            values[i], hot, (((1,), (1,)), ((), ())), preferred_element_type=F32
        )
    return total


MIDDLE = (2, 3, 4, 5)
EDGES = (0, 1, 6, 7)


def fill_middle(values, buckets, ranks, part):
    def one(g, carry):
        part[g] = in_slots(g, MIDDLE, values, buckets, ranks)
        return carry

    lax.fori_loop(0, NB // 2, one, 0)


def route_and_bin(values, buckets, ranks, out, most, part, msgs, recv, acc, tops, fin, got, sems):
    send_sem, recv_sem, fsend, frecv, own_sem = sems
    rows_me = lax.axis_index("rows")
    tm_me = lax.axis_index("tm")
    core = tm_me % 2
    chip = rows_me * 2 + tm_me // 2

    def route(i):
        rows, zh = at_offset(i)
        return pltpu.make_async_remote_copy(
            src_ref=msgs.at[i],
            dst_ref=recv.at[i],
            send_sem=send_sem.at[i],
            recv_sem=recv_sem.at[i],
            device_id=(rows, zh * 2 + core),
            device_id_type=MESH,
        )

    def fill(g):
        return (part[g] + in_slots(g, EDGES, values, buckets, ranks)).astype(BF16)

    both = fill(0)
    recv[0] = both[:, :CAP]
    msgs[1] = both[:, CAP:]
    route(1).start()

    def send(g, carry):
        both = fill(g)
        msgs[2 * g] = both[:, :CAP]
        msgs[2 * g + 1] = both[:, CAP:]
        route(2 * g).start()
        route(2 * g + 1).start()
        return carry

    lax.fori_loop(1, NB // 2, send, 0)

    acc[...] = jnp.zeros_like(acc)
    tops[...] = jnp.zeros_like(tops)
    row_id = lax.broadcasted_iota(jnp.int32, (128, 2 * CAP), 0).astype(F32)

    def add(first, second):
        both = jnp.concatenate([first, second], axis=1)
        extra = both[LAGS:MROWS].astype(F32)
        high, low = extra[0:1], extra[1:2]
        tops[...] = jnp.maximum(tops[...], extra[2:3])
        for h in range(BW // 128):
            key = jnp.where(high == h, low, -1.0)
            hot = jnp.where(row_id == key, 1.0, 0.0).astype(BF16)
            acc[:, h * 128 : (h + 1) * 128] += lax.dot_general(
                both[:LAGS], hot, (((1,), (1,)), ((), ())), preferred_element_type=F32
            )

    route(1).wait_recv()
    add(recv[0], recv[1])

    def pair(g, carry):
        i = 2 * g
        route(i).wait_recv()
        route(i + 1).wait_recv()
        add(recv[i], recv[i + 1])
        return carry

    lax.fori_loop(1, NB // 2, pair, 0)

    for h in range(BW // 128):
        fin[:, h, :] = acc[:, h * 128 : (h + 1) * 128]
    peak = jnp.max(tops[...], axis=1, keepdims=True)
    fin[:, BW // 128, :] = jnp.broadcast_to(peak, (LAGS, 128))

    half = chip // 32
    spot = core * 32 + chip % 32

    def owner(i):
        rows, zh = at_offset(i)
        return pltpu.make_async_remote_copy(
            src_ref=fin.at[rows * 2 + zh],
            dst_ref=got.at[spot],
            send_sem=fsend.at[i],
            recv_sem=frecv.at[spot],
            device_id=(rows, zh * 2 + half),
            device_id_type=MESH,
        )

    def hand(i, carry):
        owner(i).start()
        return carry

    lax.fori_loop(1, NB, hand, 0)

    own = pltpu.make_async_copy(fin.at[chip], got.at[spot], frecv.at[spot])

    @pl.when(half == core)
    def _():
        own.start()

    @pl.when(half != core)
    def _():
        owner(0).start()

    def arrived(n, carry):
        pltpu.make_async_copy(got.at[n], got.at[n], frecv.at[n]).wait()
        return carry

    lax.fori_loop(0, NB, arrived, 0)

    top = jnp.zeros((1, 128), F32)
    for j in range(32):
        out[9 * j : 9 * j + 9, :] = got[j, 0:9, :] + got[32 + j, 0:9, :]
        top = jnp.maximum(top, jnp.maximum(got[j, 9:10, :], got[32 + j, 9:10, :]))
    most[...] = jnp.broadcast_to(top, (8, 128))

    def drain(i, carry):
        route(i).wait_send()
        owner(i).wait_send()
        return carry

    lax.fori_loop(1, NB, drain, 0)

    @pl.when(half != core)
    def _():
        owner(0).wait_send()


def route_scratch():
    dma = pltpu.SemaphoreType.DMA
    return [
        pltpu.VMEM((NB // 2, MROWS, 2 * CAP), F32),
        pltpu.VMEM((NB, MROWS, CAP), BF16),
        pltpu.VMEM((NB, MROWS, CAP), BF16),
        pltpu.VMEM((LAGS, BW), F32),
        pltpu.VMEM((1, 2 * CAP), F32),
        pltpu.VMEM((LAGS, BW // 128 + 1, 128), F32),
        pltpu.VMEM((NB, BW // 128 + 1, 128), F32),
        dma((NB,)),
        dma((NB,)),
        dma((NB,)),
        dma((NB,)),
        dma(()),
    ]


SUMS = (
    jax.ShapeDtypeStruct((32 * BW // 128, 128), F32),
    jax.ShapeDtypeStruct((8, 128), F32),
)


def again_kernel(step_ref, values, labels, out, most, buckets, ranks, spread, *scratch):
    barrier = pltpu.get_barrier_semaphore()
    near = greet_near(barrier)
    x, y, z, core = position()
    signal(barrier, device(x, y, (z + 1) % 4, core))
    signal(barrier, device(x, y, (z + 3) % 4, core))
    pl.semaphore_wait(barrier, near + 2)
    for k in range(SPREAD + 1):
        spread_round(k, spread)
    fill_slots(labels, (step_ref[0, 0] * CAP).astype(F32), buckets, ranks)
    fill_middle(values, buckets, ranks, scratch[0])
    route_and_bin(values, buckets, ranks, out, most, *scratch[:7], scratch[7:])


def another_round(step, values, labels):
    return pl.pallas_call(
        again_kernel,
        out_shape=SUMS,
        in_specs=[
            pl.BlockSpec(memory_space=SMEM),
            pl.BlockSpec(memory_space=VMEM),
            pl.BlockSpec(memory_space=VMEM),
        ],
        out_specs=(pl.BlockSpec(memory_space=VMEM),) * 2,
        scratch_shapes=[
            pltpu.VMEM((ROWS8, QUARTER), F32),
            pltpu.VMEM((ROWS8, QUARTER), F32),
            pltpu.SemaphoreType.REGULAR((SPREAD,)),
            *route_scratch(),
        ],
        compiler_params=pltpu.CompilerParams(
            collective_id=1, has_side_effects=True, vmem_limit_bytes=40 << 20
        ),
        name="again",
    )(step, values, labels)


def main_kernel(
    taps, raw_in, dark_in, flat_in, gain_in, labels_in, lag_in, fhi_in, flo_in, bhi_in, blo_in,
    out, most, values_out, labels_out,
    raw, dark, flat, gain, all_labels, lag_row, fhi, flo, bhi, blo, in_sem,
    wp, smoothed, series, labels, parts, values, buckets, ranks,
    hsend, hrecv, msend, mrecv, esend, erecv, lsend, lrecv, spread, keep_sem, *scratch,
):
    rows = lax.axis_index("rows")
    tm = lax.axis_index("tm")
    over = rows + 4 - 8 * ((rows // 4) % 2)
    not_first = (rows + 31) // 32
    not_last = 1 - (rows + 1) // 32
    blocks = FB // 16

    ins = [pltpu.make_async_copy(a, b, in_sem.at[n]) for n, (a, b) in enumerate((
        (dark_in, dark), (flat_in, flat), (gain_in, gain), (labels_in, all_labels),
        (lag_in, lag_row), (fhi_in, fhi), (flo_in, flo), (bhi_in, bhi), (blo_in, blo),
    ))]
    raws = [
        pltpu.make_async_copy(raw_in.at[pl.ds(q * 16, 16)], raw.at[pl.ds(q * 16, 16)], in_sem.at[9 + q])
        for q in range(blocks)
    ]
    for copy in ins[:3]:
        copy.start()
    for copy in raws:
        copy.start()
    for copy in ins[3:]:
        copy.start()

    barrier = pltpu.get_barrier_semaphore()

    @pl.when(rows > 0)
    def _():
        signal(barrier, (rows - 1, tm))

    @pl.when(rows < 31)
    def _():
        signal(barrier, (rows + 1, tm))

    for q in range(TM):
        signal(barrier, (over, q))
    near = greet_near(barrier)

    def to_next(q):
        frames = pl.ds(pl.multiple_of(q * 16, 16), 16)
        return pltpu.make_async_remote_copy(
            src_ref=wp.at[8:10, frames], dst_ref=wp.at[0:2, frames],
            send_sem=hsend.at[0, q], recv_sem=hrecv.at[0, q],
            device_id=(rows + 1, tm), device_id_type=MESH,
        )

    def to_previous(q):
        frames = pl.ds(pl.multiple_of(q * 16, 16), 16)
        return pltpu.make_async_remote_copy(
            src_ref=wp.at[2:4, frames], dst_ref=wp.at[10:12, frames],
            send_sem=hsend.at[1, q], recv_sem=hrecv.at[1, q],
            device_id=(rows - 1, tm), device_id_type=MESH,
        )

    label_copy = pltpu.make_async_remote_copy(
        src_ref=all_labels.at[:, pl.ds(pl.multiple_of(tm * QUARTER, QUARTER), QUARTER)],
        dst_ref=labels, send_sem=lsend, recv_sem=lrecv,
        device_id=(over, tm), device_id_type=MESH,
    )

    @pl.when(rows == 0)
    def _():
        wp[0:2] = jnp.zeros((2, FB, W), BF16)

    @pl.when(rows == 31)
    def _():
        wp[10:12] = jnp.zeros((2, FB, W), BF16)

    for copy in ins[:3]:
        copy.wait()
    cols = 256
    for q in range(blocks):
        raws[q].wait()

        def weigh(c, carry):
            at = pl.ds(pl.multiple_of(c * cols, cols), cols)
            v = raw[q * 16 : (q + 1) * 16, :, at].astype(F32)
            v = (v - dark[:, at][None]) * flat[:, at][None] * gain[:, at][None]
            wp[2:10, q * 16 : (q + 1) * 16, at] = jnp.swapaxes(v, 0, 1).astype(BF16)
            return carry

        lax.fori_loop(0, W // cols, weigh, 0)

        if q == 0:
            pl.semaphore_wait(barrier, near + TM + not_first + not_last)

        @pl.when(rows < 31)
        def _():
            to_next(q).start()

        @pl.when(rows > 0)
        def _():
            to_previous(q).start()

    ins[3].wait()
    label_copy.start()

    def mine(t):
        return pl.ds(pl.multiple_of(t * FB, FB), FB)

    def across(i, q):
        return pltpu.make_async_remote_copy(
            src_ref=smoothed.at[i, :, q * QUARTER : (q + 1) * QUARTER],
            dst_ref=series.at[i, mine(tm), :],
            send_sem=msend.at[i, q], recv_sem=mrecv.at[i, tm],
            device_id=(over, q), device_id_type=MESH,
        )

    def across_edge(e, fb, q):
        return pltpu.make_async_remote_copy(
            src_ref=smoothed.at[
                pl.ds(6 * e, 2), pl.ds(pl.multiple_of(fb * 16, 16), 16), q * QUARTER : (q + 1) * QUARTER
            ],
            dst_ref=series.at[pl.ds(6 * e, 2), pl.ds(pl.multiple_of(tm * FB + fb * 16, 16), 16), :],
            send_sem=esend.at[e, fb, q], recv_sem=erecv.at[e, fb, tm],
            device_id=(over, q), device_id_type=MESH,
        )

    def middle(i, carry):
        for k in range(4):

            @pl.when(i == k + 2)
            def _():
                spread_round(k, spread)

        def one(fb, c):
            smooth_block(taps, wp, smoothed, i, fb)
            return c

        lax.fori_loop(0, blocks, one, 0)
        for q in range(TM):
            across(i, q).start()
        return carry

    lax.fori_loop(2, 6, middle, 0)

    def edges(n, carry):
        fb = n // 2
        e = n % 2
        for k in range(4, SPREAD + 1):

            @pl.when(n == 2 * (k - 4))
            def _():
                spread_round(k, spread)

        @pl.when((e == 0) & (rows > 0))
        def _():
            to_next(fb).wait_recv()

        @pl.when((e == 1) & (rows < 31))
        def _():
            to_previous(fb).wait_recv()

        def one(j, c):
            smooth_block(taps, wp, smoothed, 6 * e + j, fb)
            return c

        lax.fori_loop(0, 2, one, 0)
        for q in range(TM):
            across_edge(e, fb, q).start()
        return carry

    lax.fori_loop(0, 2 * blocks, edges, 0)

    label_copy.wait_recv()
    keep_labels = pltpu.make_async_copy(labels, labels_out, keep_sem.at[0])
    keep_labels.start()
    rounds = fill_slots(labels, 0.0, buckets, ranks, parts)

    for copy in ins[4:]:
        copy.wait()
    turned = (
        lax.broadcasted_iota(jnp.int32, (128, LAGS), 0) == lag_row[...]
    ).astype(F32).T
    pick = turned[:, :80].astype(BF16)
    lag = jnp.sum(
        turned * lax.broadcasted_iota(jnp.int32, (LAGS, 128), 1).astype(F32), axis=1, keepdims=True
    )
    chi = jnp.dot(pick, bhi[...], preferred_element_type=F32).astype(BF16)
    clo = jnp.dot(pick, blo[...], preferred_element_type=F32).astype(BF16)
    scale = 1.0 / (FRAMES - lag)
    sub = lax.broadcasted_iota(jnp.int32, (8, QUARTER), 0)

    def lags(i, carry):
        s = series[i]
        x = jnp.dot(fhi[...], s, preferred_element_type=F32)
        x = x + jnp.dot(flo[...], s, preferred_element_type=F32)
        power = x[:FPAD] * x[:FPAD] + x[FPAD:] * x[FPAD:]
        phi = power.astype(BF16)
        plo = (power - phi.astype(F32)).astype(BF16)
        r = jnp.dot(chi, phi, preferred_element_type=F32)
        r = r + jnp.dot(chi, plo, preferred_element_type=F32)
        r = r + jnp.dot(clo, phi, preferred_element_type=F32)
        r = r * scale
        extra = jnp.where(sub == 2, rounds, parts[i])
        values[i] = jnp.concatenate([r, extra], axis=0).astype(BF16)
        return carry

    def middle_lags(i, carry):
        for t in range(TM):
            part = series.at[i, pl.ds(t * FB, FB)]
            pltpu.make_async_copy(part, part, mrecv.at[i, t]).wait()
        return lags(i, carry)

    lax.fori_loop(2, 6, middle_lags, 0)
    fill_middle(values, buckets, ranks, scratch[0])

    def edge_lags(e, carry):
        for t in range(TM):
            for fb in range(blocks):
                part = series.at[pl.ds(6 * e, 2), pl.ds(t * FB + fb * 16, 16)]
                pltpu.make_async_copy(part, part, erecv.at[e, fb, t]).wait()
        lags(6 * e, carry)
        return lags(6 * e + 1, carry)

    lax.fori_loop(0, 2, edge_lags, 0)
    keep_values = pltpu.make_async_copy(values, values_out, keep_sem.at[1])
    keep_values.start()

    route_and_bin(values, buckets, ranks, out, most, *scratch[:7], scratch[7:])

    def drain(i, carry):
        for q in range(TM):
            across(i, q).wait_send()
        return carry

    lax.fori_loop(2, 6, drain, 0)

    def drain_edges(n, carry):
        for q in range(TM):
            across_edge(n % 2, n // 2, q).wait_send()
        return carry

    lax.fori_loop(0, 2 * blocks, drain_edges, 0)
    label_copy.wait_send()
    for q in range(blocks):

        @pl.when(rows < 31)
        def _():
            to_next(q).wait_send()

        @pl.when(rows > 0)
        def _():
            to_previous(q).wait_send()

    keep_labels.wait()
    keep_values.wait()


def first_round(taps, raw, dark, flat, gain, labels, lag_row, tables):
    dma = pltpu.SemaphoreType.DMA
    hbm = pl.BlockSpec(memory_space=pltpu.MemorySpace.HBM)
    vmem = pl.BlockSpec(memory_space=VMEM)
    blocks = FB // 16
    plane = (ROWS8, W)
    return pl.pallas_call(
        main_kernel,
        out_shape=(
            *SUMS,
            jax.ShapeDtypeStruct((ROWS8, MROWS, QUARTER), BF16),
            jax.ShapeDtypeStruct((ROWS8, QUARTER), jnp.int32),
        ),
        in_specs=[pl.BlockSpec(memory_space=SMEM)] + [hbm] * 10,
        out_specs=(vmem, vmem, hbm, hbm),
        scratch_shapes=[
            pltpu.VMEM((FB, ROWS8, W), BF16),
            pltpu.VMEM(plane, F32),
            pltpu.VMEM(plane, F32),
            pltpu.VMEM(plane, F32),
            pltpu.VMEM(plane, jnp.int32),
            pltpu.VMEM((1, LAGS), jnp.int32),
            pltpu.VMEM((2 * FPAD, FRAMES), BF16),
            pltpu.VMEM((2 * FPAD, FRAMES), BF16),
            pltpu.VMEM((80, FPAD), BF16),
            pltpu.VMEM((80, FPAD), BF16),
            dma((9 + blocks,)),
            pltpu.VMEM((ROWS8 + 4, FB, W), BF16),
            pltpu.VMEM((ROWS8, FB, W), BF16),
            pltpu.VMEM((ROWS8, FRAMES, QUARTER), BF16),
            pltpu.VMEM((ROWS8, QUARTER), jnp.int32),
            pltpu.VMEM((ROWS8, 8, QUARTER), F32),
            pltpu.VMEM((ROWS8, MROWS, QUARTER), BF16),
            pltpu.VMEM((ROWS8, QUARTER), F32),
            pltpu.VMEM((ROWS8, QUARTER), F32),
            dma((2, blocks)),
            dma((2, blocks)),
            dma((ROWS8, TM)),
            dma((ROWS8, TM)),
            dma((2, blocks, TM)),
            dma((2, blocks, TM)),
            dma(()),
            dma(()),
            pltpu.SemaphoreType.REGULAR((SPREAD,)),
            dma((2,)),
            *route_scratch(),
        ],
        compiler_params=pltpu.CompilerParams(
            collective_id=0, has_side_effects=True, vmem_limit_bytes=56 << 20
        ),
        name="first",
    )(taps, raw, dark, flat, gain, labels, lag_row, *tables)


def per_device(
    raw_frames, dark_frame, flat_field, pixel_gain, smoothing_kernel, bin_labels, lag_list
):
    tables = [jnp.asarray(a) for a in dft_tables()]
    sums, most, values, labels = first_round(
        smoothing_kernel, raw_frames, dark_frame, flat_field, pixel_gain, bin_labels,
        lag_list.reshape(1, LAGS), tables,
    )
    needed = most[0, 0].astype(jnp.int32)

    def more(state):
        return state[0] < needed

    def again(state):
        step, total = state
        extra, _ = another_round(step.reshape(1, 1), values, labels)
        return step + 1, total + extra

    _, sums = lax.while_loop(more, again, (jnp.int32(1), sums))
    return sums.reshape(-1)[:HALF]


def solution(mesh):
    return jax.shard_map(
        per_device,
        mesh=mesh,
        in_specs=(
            P("tm", "rows", None),
            P("rows", None),
            P("rows", None),
            P("rows", None),
            P(),
            P("rows", None),
            P(),
        ),
        out_specs=P(("rows", "tm")),
        check_vma=False,
    )
```

```python
import functools

import jax
import jax.numpy as jnp
import numpy as np
from jax import lax
from jax.experimental import pallas as pl
from jax.experimental.pallas import tpu as pltpu
from jax.sharding import PartitionSpec as P

F32 = jnp.float32
BF16 = jnp.bfloat16
MESH = pl.DeviceIdType.MESH
VMEM = pltpu.MemorySpace.VMEM
SMEM = pltpu.MemorySpace.SMEM

ROWS8 = 8
W = 2048
FB = 80
TM = 4
QUARTER = W // TM
FRAMES = FB * TM
LAGS = 64
HALF = 36000
BW = 1152
NB = 64
UNROLL = 8
CAP = 128
NDFT = 400
FPAD = 208
MROWS = 72


def dft_tables():
    t = np.arange(FRAMES)
    f = np.arange(NDFT // 2 + 1)
    angle = 2 * np.pi * ((f[:, None] * t[None, :]) % NDFT) / NDFT
    forward = np.zeros((2 * FPAD, FRAMES), np.float64)
    forward[: f.size] = np.cos(angle)
    forward[FPAD : FPAD + f.size] = np.sin(angle)
    k = np.arange(80)
    back = np.zeros((80, FPAD), np.float64)
    fold = np.full(f.size, 2.0)
    fold[0] = fold[-1] = 1.0
    back[:, : f.size] = np.cos(2 * np.pi * ((k[:, None] * f[None, :]) % NDFT) / NDFT) * fold / NDFT

    def split(a):
        hi = a.astype(jnp.bfloat16)
        lo = (a - hi.astype(np.float64)).astype(jnp.bfloat16)
        return hi, lo

    return (*split(forward), *split(back))


def position():
    rows = lax.axis_index("rows")
    tm = lax.axis_index("tm")
    return rows % 4, rows // 8, (tm // 2) * 2 + (rows // 4) % 2, tm % 2


def device(x, y, z, core):
    return (y * 8 + (z % 2) * 4 + x, (z // 2) * 2 + core)


def at_offset(i):
    x, y, z, _ = position()
    i = (i * 37) % NB
    rows, tm = device((x + i % 4) % 4, (y + (i // 4) % 4) % 4, (z + i // 16) % 4, 0)
    return rows, tm // 2


def signal(sem, where):
    pl.semaphore_signal(sem, inc=1, device_id=where, device_id_type=MESH)


def spread_partner(k):
    x, y, z, core = position()
    return (
        lambda: device(x, y, z, 1 - core),
        lambda: device((x + 1) % 4, y, z, core),
        lambda: device((x + 2) % 4, y, z, core),
        lambda: device(x, (y + 1) % 4, z, core),
        lambda: device(x, (y + 2) % 4, z, core),
        lambda: device(x, y, (z + 1) % 4, core),
        lambda: device(x, y, (z + 2) % 4, core),
    )[k]()


SPREAD = 7


def spread_round(k, sems):
    if k > 0:
        pl.semaphore_wait(sems.at[k - 1], 1)
    if k < SPREAD:
        signal(sems.at[k], spread_partner(k))


def greet_near(barrier):
    x, y, z, core = position()
    for where in (
        device(x, y, z, 1 - core),
        device((x + 1) % 4, y, z, core),
        device((x + 3) % 4, y, z, core),
        device((x + 2) % 4, y, z, core),
        device(x, (y + 1) % 4, z, core),
        device(x, (y + 3) % 4, z, core),
        device(x, (y + 2) % 4, z, core),
        device(x, y, (z + 2) % 4, core),
    ):
        signal(barrier, where)
    return 8


def smooth_block(taps, wp, out, i, fb):
    lane = lax.broadcasted_iota(jnp.int32, (16, 128), 1)
    zero = jnp.zeros((16, 128), F32)
    chunks = W // 128
    frames = pl.ds(pl.multiple_of(fb * 16, 16), 16)
    rolled = []

    def finish(c):
        left = rolled[c - 1] if c > 0 else (zero,) * 5
        right = rolled[c + 1] if c + 1 < chunks else (zero,) * 5
        mine = rolled[c]
        total = mine[2]
        total = total + jnp.where(lane >= 2, mine[0], left[0])
        total = total + jnp.where(lane >= 1, mine[1], left[1])
        total = total + jnp.where(lane < 127, mine[3], right[3])
        total = total + jnp.where(lane < 126, mine[4], right[4])
        out[i, frames, c * 128 : (c + 1) * 128] = total.astype(BF16)

    for c in range(chunks):
        rows = [wp[i + a, frames, c * 128 : (c + 1) * 128].astype(F32) for a in range(5)]
        part = []
        for b in range(5):
            acc = rows[0] * taps[0, b]
            for a in range(1, 5):
                acc = acc + rows[a] * taps[a, b]
            part.append(acc)
        rolled.append(
            (
                pltpu.roll(part[0], 2, 1),
                pltpu.roll(part[1], 1, 1),
                part[2],
                pltpu.roll(part[3], 127, 1),
                pltpu.roll(part[4], 126, 1),
            )
        )
        if c >= 1:
            finish(c - 1)
    finish(chunks - 1)


def bucket_of(label):
    half = label >= HALF
    inside = jnp.where(half, label - HALF, label)
    quotient = lax.shift_right_logical(lax.shift_right_logical(inside, 7) * 57, 9)
    bucket = jnp.where(half, quotient + 32, quotient)
    return bucket, inside - quotient * BW


def fill_slots(labels, first, buckets, ranks, parts=None):
    upper = (
        lax.broadcasted_iota(jnp.int32, (QUARTER, QUARTER), 0)
        <= lax.broadcasted_iota(jnp.int32, (QUARTER, QUARTER), 1)
    ).astype(F32).astype(BF16)
    which = lax.broadcasted_iota(jnp.int32, (NB, QUARTER), 0)
    sub = lax.broadcasted_iota(jnp.int32, (8, QUARTER), 0)
    carry = jnp.zeros((NB, 1), F32)
    for i in range(ROWS8):
        bucket, local = bucket_of(labels[i : i + 1, :])
        hot = (which == bucket).astype(F32)
        count = jnp.dot(hot.astype(BF16), upper, preferred_element_type=F32) + carry
        rank = jnp.sum(hot * count, axis=0, keepdims=True) - 1.0 - first
        ranks[i : i + 1, :] = jnp.where((rank >= 0) & (rank < CAP), rank, -1024.0)
        buckets[i : i + 1, :] = bucket.astype(F32)
        if parts is not None:
            top = lax.shift_right_logical(local, 7)
            low = local - top * 128
            parts[i] = jnp.where(sub == 0, top.astype(F32), jnp.where(sub == 1, low.astype(F32), 0.0))
        carry = count[:, QUARTER - 1 : QUARTER]
    most = jnp.max(carry, axis=0, keepdims=True)
    return lax.shift_right_logical(most.astype(jnp.int32) + (CAP - 1), 7).astype(F32)


def chip_at(i):
    rows, zh = at_offset(i)
    return (rows * 2 + zh).astype(F32)


def in_slots(g, rows, values, buckets, ranks):
    slot_id = lax.broadcasted_iota(jnp.int32, (2 * CAP, QUARTER), 0).astype(F32)
    first, second = chip_at(2 * g), chip_at(2 * g + 1)
    total = jnp.zeros((MROWS, 2 * CAP), F32)
    for i in rows:
        b = buckets[pl.ds(i, 1), :]
        r = ranks[pl.ds(i, 1), :]
        key = jnp.where(b == first, r, jnp.where(b == second, r + CAP, -1.0))
        hot = jnp.where(slot_id == key, 1.0, 0.0).astype(BF16)
        total = total + lax.dot_general(
            values[i], hot, (((1,), (1,)), ((), ())), preferred_element_type=F32
        )
    return total


MIDDLE = (2, 3, 4, 5)


def fill_part(start, stop, rows, values, buckets, ranks, part, more):
    def one(g, carry):
        total = in_slots(g, rows, values, buckets, ranks)
        part[g] = part[g] + total if more else total
        return carry

    lax.fori_loop(start, stop, one, 0, unroll=UNROLL)


def route_and_bin(last, values, buckets, ranks, out, most, part, msgs, recv, acc, tops, fin, got, sems):
    send_sem, recv_sem, fsend, frecv, own_sem = sems
    rows_me = lax.axis_index("rows")
    tm_me = lax.axis_index("tm")
    core = tm_me % 2
    chip = rows_me * 2 + tm_me // 2

    def route(i):
        rows, zh = at_offset(i)
        return pltpu.make_async_remote_copy(
            src_ref=msgs.at[i],
            dst_ref=recv.at[i],
            send_sem=send_sem.at[i],
            recv_sem=recv_sem.at[i],
            device_id=(rows, zh * 2 + core),
            device_id_type=MESH,
        )

    def fill(g):
        return (part[g] + in_slots(g, last, values, buckets, ranks)).astype(BF16)

    def send(g, carry):
        made = [fill(4 * g + u) for u in range(4)]
        for u in range(4):
            i = 2 * (4 * g + u)
            msgs[i] = made[u][:, :CAP]
            msgs[i + 1] = made[u][:, CAP:]
            if u == 0:

                @pl.when(g > 0)
                def _():
                    route(i).start()

            else:
                route(i).start()
            route(i + 1).start()
        return carry

    lax.fori_loop(0, NB // 8, send, 0)
    recv[0] = msgs[0]

    acc[...] = jnp.zeros_like(acc)
    tops[...] = jnp.zeros_like(tops)
    row_id = lax.broadcasted_iota(jnp.int32, (128, 2 * CAP), 0).astype(F32)

    def add(first, second):
        both = jnp.concatenate([first, second], axis=1)
        extra = both[LAGS:MROWS].astype(F32)
        high, low = extra[0:1], extra[1:2]
        tops[...] = jnp.maximum(tops[...], extra[2:3])
        for h in range(BW // 128):
            key = jnp.where(high == h, low, -1.0)
            hot = jnp.where(row_id == key, 1.0, 0.0).astype(BF16)
            acc[:, h * 128 : (h + 1) * 128] += lax.dot_general(
                both[:LAGS], hot, (((1,), (1,)), ((), ())), preferred_element_type=F32
            )

    route(1).wait_recv()
    add(recv[0], recv[1])

    def pair(g, carry):
        i = 2 * g
        route(i).wait_recv()
        route(i + 1).wait_recv()
        add(recv[i], recv[i + 1])
        return carry

    lax.fori_loop(1, NB // 2, pair, 0)

    for h in range(BW // 128):
        fin[:, h, :] = acc[:, h * 128 : (h + 1) * 128]
    peak = jnp.max(tops[...], axis=1, keepdims=True)
    fin[:, BW // 128, :] = jnp.broadcast_to(peak, (LAGS, 128))

    half = chip // 32
    spot = core * 32 + chip % 32

    def owner(i):
        rows, zh = at_offset(i)
        return pltpu.make_async_remote_copy(
            src_ref=fin.at[rows * 2 + zh],
            dst_ref=got.at[spot],
            send_sem=fsend.at[i],
            recv_sem=frecv.at[spot],
            device_id=(rows, zh * 2 + half),
            device_id_type=MESH,
        )

    def hand(i, carry):
        owner(i).start()
        return carry

    lax.fori_loop(1, NB, hand, 0)

    own = pltpu.make_async_copy(fin.at[chip], got.at[spot], frecv.at[spot])

    @pl.when(half == core)
    def _():
        own.start()

    @pl.when(half != core)
    def _():
        owner(0).start()

    def arrived(n, carry):
        pltpu.make_async_copy(got.at[n], got.at[n], frecv.at[n]).wait()
        return carry

    lax.fori_loop(0, NB, arrived, 0)

    top = jnp.zeros((1, 128), F32)
    for j in range(32):
        out[9 * j : 9 * j + 9, :] = got[j, 0:9, :] + got[32 + j, 0:9, :]
        top = jnp.maximum(top, jnp.maximum(got[j, 9:10, :], got[32 + j, 9:10, :]))
    most[...] = jnp.broadcast_to(top, (8, 128))

    def drain(i, carry):
        route(i).wait_send()
        owner(i).wait_send()
        return carry

    lax.fori_loop(1, NB, drain, 0)

    @pl.when(half != core)
    def _():
        owner(0).wait_send()


def route_scratch():
    dma = pltpu.SemaphoreType.DMA
    return [
        pltpu.VMEM((NB // 2, MROWS, 2 * CAP), F32),
        pltpu.VMEM((NB, MROWS, CAP), BF16),
        pltpu.VMEM((NB, MROWS, CAP), BF16),
        pltpu.VMEM((LAGS, BW), F32),
        pltpu.VMEM((1, 2 * CAP), F32),
        pltpu.VMEM((LAGS, BW // 128 + 1, 128), F32),
        pltpu.VMEM((NB, BW // 128 + 1, 128), F32),
        dma((NB,)),
        dma((NB,)),
        dma((NB,)),
        dma((NB,)),
        dma(()),
    ]


SUMS = (
    jax.ShapeDtypeStruct((32 * BW // 128, 128), F32),
    jax.ShapeDtypeStruct((8, 128), F32),
)


def again_kernel(step_ref, values, labels, out, most, buckets, ranks, spread, *scratch):
    barrier = pltpu.get_barrier_semaphore()
    near = greet_near(barrier)
    x, y, z, core = position()
    signal(barrier, device(x, y, (z + 1) % 4, core))
    signal(barrier, device(x, y, (z + 3) % 4, core))
    pl.semaphore_wait(barrier, near + 2)
    for k in range(SPREAD + 1):
        spread_round(k, spread)
    fill_slots(labels, (step_ref[0, 0] * CAP).astype(F32), buckets, ranks)
    fill_part(0, NB // 2, (0, 1) + MIDDLE, values, buckets, ranks, scratch[0], False)
    route_and_bin((6, 7), values, buckets, ranks, out, most, *scratch[:7], scratch[7:])


def another_round(step, values, labels):
    return pl.pallas_call(
        again_kernel,
        out_shape=SUMS,
        in_specs=[
            pl.BlockSpec(memory_space=SMEM),
            pl.BlockSpec(memory_space=VMEM),
            pl.BlockSpec(memory_space=VMEM),
        ],
        out_specs=(pl.BlockSpec(memory_space=VMEM),) * 2,
        scratch_shapes=[
            pltpu.VMEM((ROWS8, QUARTER), F32),
            pltpu.VMEM((ROWS8, QUARTER), F32),
            pltpu.SemaphoreType.REGULAR((SPREAD,)),
            *route_scratch(),
        ],
        compiler_params=pltpu.CompilerParams(
            collective_id=1, has_side_effects=True, vmem_limit_bytes=40 << 20
        ),
        name="again",
    )(step, values, labels)


def main_kernel(
    taps, raw_in, dark_in, flat_in, gain_in, labels_in, lag_in, fhi_in, flo_in, bhi_in, blo_in,
    out, most, values_out, labels_out,
    raw, dark, flat, gain, all_labels, lag_row, fhi, flo, bhi, blo, in_sem,
    wp, smoothed, series, labels, parts, values, buckets, ranks,
    rounds, chi, clo, scale,
    hsend, hrecv, msend, mrecv, esend, erecv, lsend, lrecv, spread, keep_sem, *scratch,
):
    rows = lax.axis_index("rows")
    tm = lax.axis_index("tm")
    over = rows + 4 - 8 * ((rows // 4) % 2)
    not_first = (rows + 31) // 32
    not_last = 1 - (rows + 1) // 32
    blocks = FB // 16

    ins = [pltpu.make_async_copy(a, b, in_sem.at[n]) for n, (a, b) in enumerate((
        (dark_in, dark), (flat_in, flat), (gain_in, gain), (labels_in, all_labels),
        (lag_in, lag_row), (fhi_in, fhi), (flo_in, flo), (bhi_in, bhi), (blo_in, blo),
    ))]
    raws = [
        pltpu.make_async_copy(raw_in.at[pl.ds(q * 16, 16)], raw.at[pl.ds(q * 16, 16)], in_sem.at[9 + q])
        for q in range(blocks)
    ]
    for copy in ins[:3]:
        copy.start()
    for copy in raws:
        copy.start()
    for copy in ins[3:]:
        copy.start()

    barrier = pltpu.get_barrier_semaphore()

    @pl.when(rows > 0)
    def _():
        signal(barrier, (rows - 1, tm))

    @pl.when(rows < 31)
    def _():
        signal(barrier, (rows + 1, tm))

    for q in range(TM):
        signal(barrier, (over, q))
    near = greet_near(barrier)

    def to_next(q):
        frames = pl.ds(pl.multiple_of(q * 16, 16), 16)
        return pltpu.make_async_remote_copy(
            src_ref=wp.at[8:10, frames], dst_ref=wp.at[0:2, frames],
            send_sem=hsend.at[0, q], recv_sem=hrecv.at[0, q],
            device_id=(rows + 1, tm), device_id_type=MESH,
        )

    def to_previous(q):
        frames = pl.ds(pl.multiple_of(q * 16, 16), 16)
        return pltpu.make_async_remote_copy(
            src_ref=wp.at[2:4, frames], dst_ref=wp.at[10:12, frames],
            send_sem=hsend.at[1, q], recv_sem=hrecv.at[1, q],
            device_id=(rows - 1, tm), device_id_type=MESH,
        )

    label_copy = pltpu.make_async_remote_copy(
        src_ref=all_labels.at[:, pl.ds(pl.multiple_of(tm * QUARTER, QUARTER), QUARTER)],
        dst_ref=labels, send_sem=lsend, recv_sem=lrecv,
        device_id=(over, tm), device_id_type=MESH,
    )

    @pl.when(rows == 0)
    def _():
        wp[0:2] = jnp.zeros((2, FB, W), BF16)

    @pl.when(rows == 31)
    def _():
        wp[10:12] = jnp.zeros((2, FB, W), BF16)

    for copy in ins[:3]:
        copy.wait()
    cols = 256
    for q in range(blocks):
        raws[q].wait()

        def weigh(c, carry):
            at = pl.ds(pl.multiple_of(c * cols, cols), cols)
            v = raw[q * 16 : (q + 1) * 16, :, at].astype(F32)
            v = (v - dark[:, at][None]) * flat[:, at][None] * gain[:, at][None]
            wp[2:10, q * 16 : (q + 1) * 16, at] = jnp.swapaxes(v, 0, 1).astype(BF16)
            return carry

        lax.fori_loop(0, W // cols, weigh, 0)

        if q == 0:
            pl.semaphore_wait(barrier, near + TM + not_first + not_last)

        @pl.when(rows < 31)
        def _():
            to_next(q).start()

        @pl.when(rows > 0)
        def _():
            to_previous(q).start()

    ins[3].wait()
    label_copy.start()

    def mine(t):
        return pl.ds(pl.multiple_of(t * FB, FB), FB)

    def across(i, q):
        return pltpu.make_async_remote_copy(
            src_ref=smoothed.at[i, :, q * QUARTER : (q + 1) * QUARTER],
            dst_ref=series.at[i, mine(tm), :],
            send_sem=msend.at[i, q], recv_sem=mrecv.at[i, tm],
            device_id=(over, q), device_id_type=MESH,
        )

    def across_edge(e, fb, q):
        return pltpu.make_async_remote_copy(
            src_ref=smoothed.at[
                pl.ds(6 * e, 2), pl.ds(pl.multiple_of(fb * 16, 16), 16), q * QUARTER : (q + 1) * QUARTER
            ],
            dst_ref=series.at[pl.ds(6 * e, 2), pl.ds(pl.multiple_of(tm * FB + fb * 16, 16), 16), :],
            send_sem=esend.at[e, fb, q], recv_sem=erecv.at[e, fb, tm],
            device_id=(over, q), device_id_type=MESH,
        )

    def middle(i, carry):
        for k in range(4):

            @pl.when(i == k + 2)
            def _():
                spread_round(k, spread)

        def one(fb, c):
            smooth_block(taps, wp, smoothed, i, fb)
            return c

        lax.fori_loop(0, blocks, one, 0)
        for q in range(TM):
            across(i, q).start()
        return carry

    lax.fori_loop(2, 6, middle, 0)

    sub = lax.broadcasted_iota(jnp.int32, (8, QUARTER), 0)
    keep_labels = pltpu.make_async_copy(labels, labels_out, keep_sem.at[0])

    def prepare():
        label_copy.wait_recv()
        keep_labels.start()
        needed = fill_slots(labels, 0.0, buckets, ranks, parts)
        rounds[...] = jnp.broadcast_to(needed, (8, 128))
        for copy in ins[4:]:
            copy.wait()
        turned = (lax.broadcasted_iota(jnp.int32, (128, LAGS), 0) == lag_row[...]).astype(F32).T
        pick = turned[:, :80].astype(BF16)
        lag = jnp.sum(
            turned * lax.broadcasted_iota(jnp.int32, (LAGS, 128), 1).astype(F32),
            axis=1, keepdims=True,
        )
        chi[...] = jnp.dot(pick, bhi[...], preferred_element_type=F32).astype(BF16)
        clo[...] = jnp.dot(pick, blo[...], preferred_element_type=F32).astype(BF16)
        scale[...] = jnp.broadcast_to(1.0 / (FRAMES - lag), (LAGS, 128))

    def lags(i):
        s = series[i]
        x = jnp.dot(fhi[...], s, preferred_element_type=F32)
        x = x + jnp.dot(flo[...], s, preferred_element_type=F32)
        power = x[:FPAD] * x[:FPAD] + x[FPAD:] * x[FPAD:]
        phi = power.astype(BF16)
        plo = (power - phi.astype(F32)).astype(BF16)
        r = jnp.dot(chi[...], phi, preferred_element_type=F32)
        r = r + jnp.dot(chi[...], plo, preferred_element_type=F32)
        r = r + jnp.dot(clo[...], phi, preferred_element_type=F32)
        r = r * scale[:, :1]
        extra = jnp.where(sub == 2, rounds[:1, :1], parts[i])
        values[i] = jnp.concatenate([r, extra], axis=0).astype(BF16)

    def middle_lags(i):
        for t in range(TM):
            part = series.at[i, pl.ds(t * FB, FB)]
            pltpu.make_async_copy(part, part, mrecv.at[i, t]).wait()
        lags(i)

    def edge_lags(e):
        for t in range(TM):
            for fb in range(blocks):
                part = series.at[pl.ds(6 * e, 2), pl.ds(t * FB + fb * 16, 16)]
                pltpu.make_async_copy(part, part, erecv.at[e, fb, t]).wait()

        def one(j, c):
            lags(6 * e + j)
            return c

        lax.fori_loop(0, 2, one, 0)

    flip = 1 - (rows % 4 + 3) // 4

    def edges(n, carry):
        fb = n % blocks
        e = (n // blocks + flip) % 2
        for k in range(4, SPREAD + 1):

            @pl.when(n == k - 4)
            def _():
                spread_round(k, spread)

        @pl.when((e == 0) & (rows > 0))
        def _():
            to_next(fb).wait_recv()

        @pl.when((e == 1) & (rows < 31))
        def _():
            to_previous(fb).wait_recv()

        def one(j, c):
            smooth_block(taps, wp, smoothed, 6 * e + j, fb)
            return c

        lax.fori_loop(0, 2, one, 0)
        for q in range(TM):
            across_edge(e, fb, q).start()

        @pl.when(n == 0)
        def _():
            prepare()

        return carry

    lax.fori_loop(0, 2 * blocks, edges, 0)

    def middle(i, carry):
        middle_lags(i)
        return carry

    lax.fori_loop(2, 6, middle, 0)
    fill_part(0, NB // 2, MIDDLE, values, buckets, ranks, scratch[0], False)
    edge_lags(flip)
    fill_part(0, NB // 2, (6 * flip, 6 * flip + 1), values, buckets, ranks, scratch[0], True)
    last = 1 - flip
    edge_lags(last)
    keep_values = pltpu.make_async_copy(values, values_out, keep_sem.at[1])
    keep_values.start()

    route_and_bin((6 * last, 6 * last + 1), values, buckets, ranks, out, most, *scratch[:7], scratch[7:])

    def drain(i, carry):
        for q in range(TM):
            across(i, q).wait_send()
        return carry

    lax.fori_loop(2, 6, drain, 0)

    def drain_edges(n, carry):
        for q in range(TM):
            across_edge(n % 2, n // 2, q).wait_send()
        return carry

    lax.fori_loop(0, 2 * blocks, drain_edges, 0)
    label_copy.wait_send()
    for q in range(blocks):

        @pl.when(rows < 31)
        def _():
            to_next(q).wait_send()

        @pl.when(rows > 0)
        def _():
            to_previous(q).wait_send()

    keep_labels.wait()
    keep_values.wait()


def first_round(taps, raw, dark, flat, gain, labels, lag_row, tables):
    dma = pltpu.SemaphoreType.DMA
    hbm = pl.BlockSpec(memory_space=pltpu.MemorySpace.HBM)
    vmem = pl.BlockSpec(memory_space=VMEM)
    blocks = FB // 16
    plane = (ROWS8, W)
    return pl.pallas_call(
        main_kernel,
        out_shape=(
            *SUMS,
            jax.ShapeDtypeStruct((ROWS8, MROWS, QUARTER), BF16),
            jax.ShapeDtypeStruct((ROWS8, QUARTER), jnp.int32),
        ),
        in_specs=[pl.BlockSpec(memory_space=SMEM)] + [hbm] * 10,
        out_specs=(vmem, vmem, hbm, hbm),
        scratch_shapes=[
            pltpu.VMEM((FB, ROWS8, W), BF16),
            pltpu.VMEM(plane, F32),
            pltpu.VMEM(plane, F32),
            pltpu.VMEM(plane, F32),
            pltpu.VMEM(plane, jnp.int32),
            pltpu.VMEM((1, LAGS), jnp.int32),
            pltpu.VMEM((2 * FPAD, FRAMES), BF16),
            pltpu.VMEM((2 * FPAD, FRAMES), BF16),
            pltpu.VMEM((80, FPAD), BF16),
            pltpu.VMEM((80, FPAD), BF16),
            dma((9 + blocks,)),
            pltpu.VMEM((ROWS8 + 4, FB, W), BF16),
            pltpu.VMEM((ROWS8, FB, W), BF16),
            pltpu.VMEM((ROWS8, FRAMES, QUARTER), BF16),
            pltpu.VMEM((ROWS8, QUARTER), jnp.int32),
            pltpu.VMEM((ROWS8, 8, QUARTER), F32),
            pltpu.VMEM((ROWS8, MROWS, QUARTER), BF16),
            pltpu.VMEM((ROWS8, QUARTER), F32),
            pltpu.VMEM((ROWS8, QUARTER), F32),
            pltpu.VMEM((8, 128), F32),
            pltpu.VMEM((LAGS, FPAD), BF16),
            pltpu.VMEM((LAGS, FPAD), BF16),
            pltpu.VMEM((LAGS, 128), F32),
            dma((2, blocks)),
            dma((2, blocks)),
            dma((ROWS8, TM)),
            dma((ROWS8, TM)),
            dma((2, blocks, TM)),
            dma((2, blocks, TM)),
            dma(()),
            dma(()),
            pltpu.SemaphoreType.REGULAR((SPREAD,)),
            dma((2,)),
            *route_scratch(),
        ],
        compiler_params=pltpu.CompilerParams(
            collective_id=0, has_side_effects=True, vmem_limit_bytes=56 << 20
        ),
        name="first",
    )(taps, raw, dark, flat, gain, labels, lag_row, *tables)


def per_device(
    raw_frames, dark_frame, flat_field, pixel_gain, smoothing_kernel, bin_labels, lag_list
):
    tables = [jnp.asarray(a) for a in dft_tables()]
    sums, most, values, labels = first_round(
        smoothing_kernel, raw_frames, dark_frame, flat_field, pixel_gain, bin_labels,
        lag_list.reshape(1, LAGS), tables,
    )
    needed = most[0, 0].astype(jnp.int32)

    def more(state):
        return state[0] < needed

    def again(state):
        step, total = state
        extra, _ = another_round(step.reshape(1, 1), values, labels)
        return step + 1, total + extra

    _, sums = lax.while_loop(more, again, (jnp.int32(1), sums))
    return sums.reshape(-1)[:HALF]


def solution(mesh):
    return jax.shard_map(
        per_device,
        mesh=mesh,
        in_specs=(
            P("tm", "rows", None),
            P("rows", None),
            P("rows", None),
            P("rows", None),
            P(),
            P("rows", None),
            P(),
        ),
        out_specs=P(("rows", "tm")),
        check_vma=False,
    )
```

```python
import functools

import jax
import jax.numpy as jnp
import numpy as np
from jax import lax
from jax.experimental import pallas as pl
from jax.experimental.pallas import tpu as pltpu
from jax.sharding import PartitionSpec as P

F32 = jnp.float32
BF16 = jnp.bfloat16
MESH = pl.DeviceIdType.MESH
VMEM = pltpu.MemorySpace.VMEM
SMEM = pltpu.MemorySpace.SMEM

ROWS8 = 8
W = 2048
FB = 80
TM = 4
QUARTER = W // TM
FRAMES = FB * TM
LAGS = 64
HALF = 36000
BW = 1152
NB = 64
UNROLL = 8
CAP = 128
NDFT = 400
FPAD = 208
MROWS = 72


def dft_tables():
    t = np.arange(FRAMES)
    f = np.arange(NDFT // 2 + 1)
    angle = 2 * np.pi * ((f[:, None] * t[None, :]) % NDFT) / NDFT
    forward = np.zeros((2 * FPAD, FRAMES), np.float64)
    forward[: f.size] = np.cos(angle)
    forward[FPAD : FPAD + f.size] = np.sin(angle)
    k = np.arange(80)
    back = np.zeros((80, FPAD), np.float64)
    fold = np.full(f.size, 2.0)
    fold[0] = fold[-1] = 1.0
    back[:, : f.size] = np.cos(2 * np.pi * ((k[:, None] * f[None, :]) % NDFT) / NDFT) * fold / NDFT

    def split(a):
        hi = a.astype(jnp.bfloat16)
        lo = (a - hi.astype(np.float64)).astype(jnp.bfloat16)
        return hi, lo

    return (*split(forward), *split(back))


def position():
    rows = lax.axis_index("rows")
    tm = lax.axis_index("tm")
    return rows % 4, rows // 8, (tm // 2) * 2 + (rows // 4) % 2, tm % 2


def device(x, y, z, core):
    return (y * 8 + (z % 2) * 4 + x, (z // 2) * 2 + core)


def at_offset(i):
    x, y, z, _ = position()
    i = (i * 37) % NB
    rows, tm = device((x + i % 4) % 4, (y + (i // 4) % 4) % 4, (z + i // 16) % 4, 0)
    return rows, tm // 2


def signal(sem, where):
    pl.semaphore_signal(sem, inc=1, device_id=where, device_id_type=MESH)


def spread_partner(k):
    x, y, z, core = position()
    return (
        lambda: device(x, y, z, 1 - core),
        lambda: device((x + 1) % 4, y, z, core),
        lambda: device((x + 2) % 4, y, z, core),
        lambda: device(x, (y + 1) % 4, z, core),
        lambda: device(x, (y + 2) % 4, z, core),
        lambda: device(x, y, (z + 1) % 4, core),
        lambda: device(x, y, (z + 2) % 4, core),
    )[k]()


SPREAD = 7


def spread_round(k, sems):
    if k > 0:
        pl.semaphore_wait(sems.at[k - 1], 1)
    if k < SPREAD:
        signal(sems.at[k], spread_partner(k))


def greet_near(barrier):
    x, y, z, core = position()
    for where in (
        device(x, y, z, 1 - core),
        device((x + 1) % 4, y, z, core),
        device((x + 3) % 4, y, z, core),
        device((x + 2) % 4, y, z, core),
        device(x, (y + 1) % 4, z, core),
        device(x, (y + 3) % 4, z, core),
        device(x, (y + 2) % 4, z, core),
        device(x, y, (z + 2) % 4, core),
    ):
        signal(barrier, where)
    return 8


def smooth_block(taps, wp, out, i, fb):
    lane = lax.broadcasted_iota(jnp.int32, (16, 128), 1)
    zero = jnp.zeros((16, 128), F32)
    chunks = W // 128
    frames = pl.ds(pl.multiple_of(fb * 16, 16), 16)
    rolled = []

    def finish(c):
        left = rolled[c - 1] if c > 0 else (zero,) * 5
        right = rolled[c + 1] if c + 1 < chunks else (zero,) * 5
        mine = rolled[c]
        total = mine[2]
        total = total + jnp.where(lane >= 2, mine[0], left[0])
        total = total + jnp.where(lane >= 1, mine[1], left[1])
        total = total + jnp.where(lane < 127, mine[3], right[3])
        total = total + jnp.where(lane < 126, mine[4], right[4])
        out[i, frames, c * 128 : (c + 1) * 128] = total.astype(BF16)

    for c in range(chunks):
        rows = [wp[i + a, frames, c * 128 : (c + 1) * 128].astype(F32) for a in range(5)]
        part = []
        for b in range(5):
            acc = rows[0] * taps[0, b]
            for a in range(1, 5):
                acc = acc + rows[a] * taps[a, b]
            part.append(acc)
        rolled.append(
            (
                pltpu.roll(part[0], 2, 1),
                pltpu.roll(part[1], 1, 1),
                part[2],
                pltpu.roll(part[3], 127, 1),
                pltpu.roll(part[4], 126, 1),
            )
        )
        if c >= 1:
            finish(c - 1)
    finish(chunks - 1)


def bucket_of(label):
    half = label >= HALF
    inside = jnp.where(half, label - HALF, label)
    quotient = lax.shift_right_logical(lax.shift_right_logical(inside, 7) * 57, 9)
    bucket = jnp.where(half, quotient + 32, quotient)
    return bucket, inside - quotient * BW


def fill_slots(labels, first, buckets, ranks, parts=None):
    upper = (
        lax.broadcasted_iota(jnp.int32, (QUARTER, QUARTER), 0)
        <= lax.broadcasted_iota(jnp.int32, (QUARTER, QUARTER), 1)
    ).astype(F32).astype(BF16)
    which = lax.broadcasted_iota(jnp.int32, (NB, QUARTER), 0)
    sub = lax.broadcasted_iota(jnp.int32, (8, QUARTER), 0)
    carry = jnp.zeros((NB, 1), F32)
    for i in range(ROWS8):
        bucket, local = bucket_of(labels[i : i + 1, :])
        hot = (which == bucket).astype(F32)
        count = jnp.dot(hot.astype(BF16), upper, preferred_element_type=F32) + carry
        rank = jnp.sum(hot * count, axis=0, keepdims=True) - 1.0 - first
        ranks[i : i + 1, :] = jnp.where((rank >= 0) & (rank < CAP), rank, -1024.0)
        buckets[i : i + 1, :] = bucket.astype(F32)
        if parts is not None:
            top = lax.shift_right_logical(local, 7)
            low = local - top * 128
            parts[i] = jnp.where(sub == 0, top.astype(F32), jnp.where(sub == 1, low.astype(F32), 0.0))
        carry = count[:, QUARTER - 1 : QUARTER]
    most = jnp.max(carry, axis=0, keepdims=True)
    return lax.shift_right_logical(most.astype(jnp.int32) + (CAP - 1), 7).astype(F32)


def chip_at(i):
    rows, zh = at_offset(i)
    return (rows * 2 + zh).astype(F32)


def in_slots(g, rows, values, buckets, ranks):
    slot_id = lax.broadcasted_iota(jnp.int32, (2 * CAP, QUARTER), 0).astype(F32)
    first, second = chip_at(2 * g), chip_at(2 * g + 1)
    total = jnp.zeros((MROWS, 2 * CAP), F32)
    for i in rows:
        b = buckets[pl.ds(i, 1), :]
        r = ranks[pl.ds(i, 1), :]
        key = jnp.where(b == first, r, jnp.where(b == second, r + CAP, -1.0))
        hot = jnp.where(slot_id == key, 1.0, 0.0).astype(BF16)
        total = total + lax.dot_general(
            values[i], hot, (((1,), (1,)), ((), ())), preferred_element_type=F32
        )
    return total


MIDDLE = (2, 3, 4, 5)


def fill_part(start, stop, rows, values, buckets, ranks, part, more):
    def one(g, carry):
        total = in_slots(g, rows, values, buckets, ranks)
        part[g] = part[g] + total if more else total
        return carry

    lax.fori_loop(start, stop, one, 0, unroll=UNROLL)


def route_and_bin(last, values, buckets, ranks, out, most, part, msgs, recv, acc, tops, fin, got, sems):
    send_sem, recv_sem, fsend, frecv, own_sem = sems
    rows_me = lax.axis_index("rows")
    tm_me = lax.axis_index("tm")
    core = tm_me % 2
    chip = rows_me * 2 + tm_me // 2

    def route(i):
        rows, zh = at_offset(i)
        return pltpu.make_async_remote_copy(
            src_ref=msgs.at[i],
            dst_ref=recv.at[i],
            send_sem=send_sem.at[i],
            recv_sem=recv_sem.at[i],
            device_id=(rows, zh * 2 + core),
            device_id_type=MESH,
        )

    def fill(g):
        return (part[g] + in_slots(g, last, values, buckets, ranks)).astype(BF16)

    def send(g, carry):
        made = [fill(4 * g + u) for u in range(4)]
        for u in range(4):
            i = 2 * (4 * g + u)
            msgs[i] = made[u][:, :CAP]
            msgs[i + 1] = made[u][:, CAP:]
            if u == 0:

                @pl.when(g > 0)
                def _():
                    route(i).start()

            else:
                route(i).start()
            route(i + 1).start()
        return carry

    lax.fori_loop(0, NB // 8, send, 0)
    recv[0] = msgs[0]

    acc[...] = jnp.zeros_like(acc)
    tops[...] = jnp.zeros_like(tops)
    row_id = lax.broadcasted_iota(jnp.int32, (128, 2 * CAP), 0).astype(F32)

    def add(first, second):
        both = jnp.concatenate([first, second], axis=1)
        extra = both[LAGS:MROWS].astype(F32)
        high, low = extra[0:1], extra[1:2]
        tops[...] = jnp.maximum(tops[...], extra[2:3])
        for h in range(0, BW // 128, 2):
            width = min(256, BW - h * 128)
            hot = jnp.concatenate(
                [
                    jnp.where(row_id == jnp.where(high == h + u, low, -1.0), 1.0, 0.0).astype(BF16)
                    for u in range(width // 128)
                ],
                axis=0,
            )
            acc[:, h * 128 : h * 128 + width] += lax.dot_general(
                both[:LAGS], hot, (((1,), (1,)), ((), ())), preferred_element_type=F32
            )

    def pairs(h, carry):
        for u in range(8):
            i = 8 * h + u
            if u == 0:

                @pl.when(h > 0)
                def _():
                    route(i).wait_recv()

            else:
                route(i).wait_recv()
        for u in range(4):
            add(recv[8 * h + 2 * u], recv[8 * h + 2 * u + 1])
        return carry

    lax.fori_loop(0, NB // 8, pairs, 0)

    for h in range(BW // 128):
        fin[:, h, :] = acc[:, h * 128 : (h + 1) * 128]
    peak = jnp.max(tops[...], axis=1, keepdims=True)
    fin[:, BW // 128, :] = jnp.broadcast_to(peak, (LAGS, 128))

    half = chip // 32
    spot = core * 32 + chip % 32

    def owner(i):
        rows, zh = at_offset(i)
        return pltpu.make_async_remote_copy(
            src_ref=fin.at[rows * 2 + zh],
            dst_ref=got.at[spot],
            send_sem=fsend.at[i],
            recv_sem=frecv.at[spot],
            device_id=(rows, zh * 2 + half),
            device_id_type=MESH,
        )

    def hand(i, carry):
        owner(i).start()
        return carry

    lax.fori_loop(1, NB, hand, 0)

    own = pltpu.make_async_copy(fin.at[chip], got.at[spot], frecv.at[spot])

    @pl.when(half == core)
    def _():
        own.start()

    @pl.when(half != core)
    def _():
        owner(0).start()

    def arrived(n, carry):
        pltpu.make_async_copy(got.at[n], got.at[n], frecv.at[n]).wait()
        return carry

    lax.fori_loop(0, NB, arrived, 0)

    top = jnp.zeros((1, 128), F32)
    for j in range(32):
        out[9 * j : 9 * j + 9, :] = got[j, 0:9, :] + got[32 + j, 0:9, :]
        top = jnp.maximum(top, jnp.maximum(got[j, 9:10, :], got[32 + j, 9:10, :]))
    most[0, 0] = jnp.max(top).astype(jnp.int32)

    def drain(i, carry):
        route(i).wait_send()
        owner(i).wait_send()
        return carry

    lax.fori_loop(1, NB, drain, 0)

    @pl.when(half != core)
    def _():
        owner(0).wait_send()


def route_scratch():
    dma = pltpu.SemaphoreType.DMA
    return [
        pltpu.VMEM((NB // 2, MROWS, 2 * CAP), F32),
        pltpu.VMEM((NB, MROWS, CAP), BF16),
        pltpu.VMEM((NB, MROWS, CAP), BF16),
        pltpu.VMEM((LAGS, BW), F32),
        pltpu.VMEM((1, 2 * CAP), F32),
        pltpu.VMEM((LAGS, BW // 128 + 1, 128), F32),
        pltpu.VMEM((NB, BW // 128 + 1, 128), F32),
        dma((NB,)),
        dma((NB,)),
        dma((NB,)),
        dma((NB,)),
        dma(()),
    ]


SUMS = (
    jax.ShapeDtypeStruct((32 * BW // 128, 128), F32),
    jax.ShapeDtypeStruct((1, 1), jnp.int32),
)


def again_kernel(step_ref, values, labels, out, most, buckets, ranks, spread, *scratch):
    barrier = pltpu.get_barrier_semaphore()
    near = greet_near(barrier)
    x, y, z, core = position()
    signal(barrier, device(x, y, (z + 1) % 4, core))
    signal(barrier, device(x, y, (z + 3) % 4, core))
    pl.semaphore_wait(barrier, near + 2)
    for k in range(SPREAD + 1):
        spread_round(k, spread)
    fill_slots(labels, (step_ref[0, 0] * CAP).astype(F32), buckets, ranks)
    fill_part(0, NB // 2, (0, 1) + MIDDLE, values, buckets, ranks, scratch[0], False)
    route_and_bin((6, 7), values, buckets, ranks, out, most, *scratch[:7], scratch[7:])


def another_round(step, values, labels):
    return pl.pallas_call(
        again_kernel,
        out_shape=SUMS,
        in_specs=[
            pl.BlockSpec(memory_space=SMEM),
            pl.BlockSpec(memory_space=VMEM),
            pl.BlockSpec(memory_space=VMEM),
        ],
        out_specs=(pl.BlockSpec(memory_space=VMEM), pl.BlockSpec(memory_space=SMEM)),
        scratch_shapes=[
            pltpu.VMEM((ROWS8, QUARTER), F32),
            pltpu.VMEM((ROWS8, QUARTER), F32),
            pltpu.SemaphoreType.REGULAR((SPREAD,)),
            *route_scratch(),
        ],
        compiler_params=pltpu.CompilerParams(
            collective_id=1, has_side_effects=True, vmem_limit_bytes=40 << 20
        ),
        name="again",
    )(step, values, labels)


def main_kernel(
    taps, raw_in, dark_in, flat_in, gain_in, labels_in, lag_in, fhi_in, flo_in, bhi_in, blo_in,
    out, most, values_out, labels_out,
    raw, dark, flat, gain, all_labels, lag_row, fhi, flo, bhi, blo, in_sem,
    wp, smoothed, series, labels, parts, values, buckets, ranks,
    rounds, chi, clo, scale,
    hsend, hrecv, msend, mrecv, esend, erecv, lsend, lrecv, spread, keep_sem, *scratch,
):
    rows = lax.axis_index("rows")
    tm = lax.axis_index("tm")
    over = rows + 4 - 8 * ((rows // 4) % 2)
    not_first = (rows + 31) // 32
    not_last = 1 - (rows + 1) // 32
    blocks = FB // 16

    ins = [pltpu.make_async_copy(a, b, in_sem.at[n]) for n, (a, b) in enumerate((
        (dark_in, dark), (flat_in, flat), (gain_in, gain), (labels_in, all_labels),
        (lag_in, lag_row), (fhi_in, fhi), (flo_in, flo), (bhi_in, bhi), (blo_in, blo),
    ))]
    raws = [
        pltpu.make_async_copy(raw_in.at[pl.ds(q * 16, 16)], raw.at[pl.ds(q * 16, 16)], in_sem.at[9 + q])
        for q in range(blocks)
    ]
    for copy in ins[:3]:
        copy.start()
    for copy in raws:
        copy.start()
    for copy in ins[3:]:
        copy.start()

    barrier = pltpu.get_barrier_semaphore()

    @pl.when(rows > 0)
    def _():
        signal(barrier, (rows - 1, tm))

    @pl.when(rows < 31)
    def _():
        signal(barrier, (rows + 1, tm))

    for q in range(TM):
        signal(barrier, (over, q))
    near = greet_near(barrier)

    def to_next(q):
        frames = pl.ds(pl.multiple_of(q * 16, 16), 16)
        return pltpu.make_async_remote_copy(
            src_ref=wp.at[8:10, frames], dst_ref=wp.at[0:2, frames],
            send_sem=hsend.at[0, q], recv_sem=hrecv.at[0, q],
            device_id=(rows + 1, tm), device_id_type=MESH,
        )

    def to_previous(q):
        frames = pl.ds(pl.multiple_of(q * 16, 16), 16)
        return pltpu.make_async_remote_copy(
            src_ref=wp.at[2:4, frames], dst_ref=wp.at[10:12, frames],
            send_sem=hsend.at[1, q], recv_sem=hrecv.at[1, q],
            device_id=(rows - 1, tm), device_id_type=MESH,
        )

    label_copy = pltpu.make_async_remote_copy(
        src_ref=all_labels.at[:, pl.ds(pl.multiple_of(tm * QUARTER, QUARTER), QUARTER)],
        dst_ref=labels, send_sem=lsend, recv_sem=lrecv,
        device_id=(over, tm), device_id_type=MESH,
    )

    @pl.when(rows == 0)
    def _():
        wp[0:2] = jnp.zeros((2, FB, W), BF16)

    @pl.when(rows == 31)
    def _():
        wp[10:12] = jnp.zeros((2, FB, W), BF16)

    for copy in ins[:3]:
        copy.wait()
    cols = 256
    for q in range(blocks):
        raws[q].wait()

        def weigh(c, carry):
            at = pl.ds(pl.multiple_of(c * cols, cols), cols)
            v = raw[q * 16 : (q + 1) * 16, :, at].astype(F32)
            v = (v - dark[:, at][None]) * flat[:, at][None] * gain[:, at][None]
            wp[2:10, q * 16 : (q + 1) * 16, at] = jnp.swapaxes(v, 0, 1).astype(BF16)
            return carry

        lax.fori_loop(0, W // cols, weigh, 0)

        if q == 0:
            pl.semaphore_wait(barrier, near + TM + not_first + not_last)

        @pl.when(rows < 31)
        def _():
            to_next(q).start()

        @pl.when(rows > 0)
        def _():
            to_previous(q).start()

    ins[3].wait()
    label_copy.start()

    def mine(t):
        return pl.ds(pl.multiple_of(t * FB, FB), FB)

    def across(i, q):
        return pltpu.make_async_remote_copy(
            src_ref=smoothed.at[i, :, q * QUARTER : (q + 1) * QUARTER],
            dst_ref=series.at[i, mine(tm), :],
            send_sem=msend.at[i, q], recv_sem=mrecv.at[i, tm],
            device_id=(over, q), device_id_type=MESH,
        )

    def across_edge(e, fb, q):
        return pltpu.make_async_remote_copy(
            src_ref=smoothed.at[
                pl.ds(6 * e, 2), pl.ds(pl.multiple_of(fb * 16, 16), 16), q * QUARTER : (q + 1) * QUARTER
            ],
            dst_ref=series.at[pl.ds(6 * e, 2), pl.ds(pl.multiple_of(tm * FB + fb * 16, 16), 16), :],
            send_sem=esend.at[e, fb, q], recv_sem=erecv.at[e, fb, tm],
            device_id=(over, q), device_id_type=MESH,
        )

    def middle(i, carry):
        for k in range(4):

            @pl.when(i == k + 2)
            def _():
                spread_round(k, spread)

        def one(fb, c):
            smooth_block(taps, wp, smoothed, i, fb)
            return c

        lax.fori_loop(0, blocks, one, 0)
        for q in range(TM):
            across(i, q).start()
        return carry

    lax.fori_loop(2, 6, middle, 0)

    sub = lax.broadcasted_iota(jnp.int32, (8, QUARTER), 0)
    keep_labels = pltpu.make_async_copy(labels, labels_out, keep_sem.at[0])

    def prepare():
        label_copy.wait_recv()
        keep_labels.start()
        needed = fill_slots(labels, 0.0, buckets, ranks, parts)
        rounds[...] = jnp.broadcast_to(needed, (8, 128))
        for copy in ins[4:]:
            copy.wait()
        turned = (lax.broadcasted_iota(jnp.int32, (128, LAGS), 0) == lag_row[...]).astype(F32).T
        pick = turned[:, :80].astype(BF16)
        lag = jnp.sum(
            turned * lax.broadcasted_iota(jnp.int32, (LAGS, 128), 1).astype(F32),
            axis=1, keepdims=True,
        )
        chi[...] = jnp.dot(pick, bhi[...], preferred_element_type=F32).astype(BF16)
        clo[...] = jnp.dot(pick, blo[...], preferred_element_type=F32).astype(BF16)
        scale[...] = jnp.broadcast_to(1.0 / (FRAMES - lag), (LAGS, 128))

    def lags(i):
        s = series[i]
        x = jnp.dot(fhi[...], s, preferred_element_type=F32)
        x = x + jnp.dot(flo[...], s, preferred_element_type=F32)
        power = x[:FPAD] * x[:FPAD] + x[FPAD:] * x[FPAD:]
        phi = power.astype(BF16)
        plo = (power - phi.astype(F32)).astype(BF16)
        r = jnp.dot(chi[...], phi, preferred_element_type=F32)
        r = r + jnp.dot(chi[...], plo, preferred_element_type=F32)
        r = r + jnp.dot(clo[...], phi, preferred_element_type=F32)
        r = r * scale[:, :1]
        extra = jnp.where(sub == 2, rounds[:1, :1], parts[i])
        values[i] = jnp.concatenate([r, extra], axis=0).astype(BF16)

    def middle_lags(i):
        for t in range(TM):
            part = series.at[i, pl.ds(t * FB, FB)]
            pltpu.make_async_copy(part, part, mrecv.at[i, t]).wait()
        lags(i)

    def edge_lags(e):
        for t in range(TM):
            for fb in range(blocks):
                part = series.at[pl.ds(6 * e, 2), pl.ds(t * FB + fb * 16, 16)]
                pltpu.make_async_copy(part, part, erecv.at[e, fb, t]).wait()

        def one(j, c):
            lags(6 * e + j)
            return c

        lax.fori_loop(0, 2, one, 0)

    flip = 1 - (rows % 4 + 3) // 4

    def edges(n, carry):
        fb = n % blocks
        e = (n // blocks + flip) % 2
        for k in range(4, SPREAD + 1):

            @pl.when(n == k - 4)
            def _():
                spread_round(k, spread)

        @pl.when((e == 0) & (rows > 0))
        def _():
            to_next(fb).wait_recv()

        @pl.when((e == 1) & (rows < 31))
        def _():
            to_previous(fb).wait_recv()

        def one(j, c):
            smooth_block(taps, wp, smoothed, 6 * e + j, fb)
            return c

        lax.fori_loop(0, 2, one, 0)
        for q in range(TM):
            across_edge(e, fb, q).start()

        @pl.when(n == 0)
        def _():
            prepare()

        return carry

    lax.fori_loop(0, 2 * blocks, edges, 0)

    def middle(i, carry):
        middle_lags(i)
        return carry

    lax.fori_loop(2, 6, middle, 0)
    fill_part(0, NB // 2, MIDDLE, values, buckets, ranks, scratch[0], False)
    edge_lags(flip)
    fill_part(0, NB // 2, (6 * flip, 6 * flip + 1), values, buckets, ranks, scratch[0], True)
    last = 1 - flip
    edge_lags(last)
    keep_values = pltpu.make_async_copy(values, values_out, keep_sem.at[1])
    keep_values.start()

    route_and_bin((6 * last, 6 * last + 1), values, buckets, ranks, out, most, *scratch[:7], scratch[7:])

    def drain(i, carry):
        for q in range(TM):
            across(i, q).wait_send()
        return carry

    lax.fori_loop(2, 6, drain, 0)

    def drain_edges(n, carry):
        for q in range(TM):
            across_edge(n % 2, n // 2, q).wait_send()
        return carry

    lax.fori_loop(0, 2 * blocks, drain_edges, 0)
    label_copy.wait_send()
    for q in range(blocks):

        @pl.when(rows < 31)
        def _():
            to_next(q).wait_send()

        @pl.when(rows > 0)
        def _():
            to_previous(q).wait_send()

    keep_labels.wait()
    keep_values.wait()


def first_round(taps, raw, dark, flat, gain, labels, lag_row, tables):
    dma = pltpu.SemaphoreType.DMA
    hbm = pl.BlockSpec(memory_space=pltpu.MemorySpace.HBM)
    vmem = pl.BlockSpec(memory_space=VMEM)
    blocks = FB // 16
    plane = (ROWS8, W)
    return pl.pallas_call(
        main_kernel,
        out_shape=(
            *SUMS,
            jax.ShapeDtypeStruct((ROWS8, MROWS, QUARTER), BF16),
            jax.ShapeDtypeStruct((ROWS8, QUARTER), jnp.int32),
        ),
        in_specs=[pl.BlockSpec(memory_space=SMEM)] + [hbm] * 10,
        out_specs=(vmem, pl.BlockSpec(memory_space=SMEM), hbm, hbm),
        scratch_shapes=[
            pltpu.VMEM((FB, ROWS8, W), BF16),
            pltpu.VMEM(plane, F32),
            pltpu.VMEM(plane, F32),
            pltpu.VMEM(plane, F32),
            pltpu.VMEM(plane, jnp.int32),
            pltpu.VMEM((1, LAGS), jnp.int32),
            pltpu.VMEM((2 * FPAD, FRAMES), BF16),
            pltpu.VMEM((2 * FPAD, FRAMES), BF16),
            pltpu.VMEM((80, FPAD), BF16),
            pltpu.VMEM((80, FPAD), BF16),
            dma((9 + blocks,)),
            pltpu.VMEM((ROWS8 + 4, FB, W), BF16),
            pltpu.VMEM((ROWS8, FB, W), BF16),
            pltpu.VMEM((ROWS8, FRAMES, QUARTER), BF16),
            pltpu.VMEM((ROWS8, QUARTER), jnp.int32),
            pltpu.VMEM((ROWS8, 8, QUARTER), F32),
            pltpu.VMEM((ROWS8, MROWS, QUARTER), BF16),
            pltpu.VMEM((ROWS8, QUARTER), F32),
            pltpu.VMEM((ROWS8, QUARTER), F32),
            pltpu.VMEM((8, 128), F32),
            pltpu.VMEM((LAGS, FPAD), BF16),
            pltpu.VMEM((LAGS, FPAD), BF16),
            pltpu.VMEM((LAGS, 128), F32),
            dma((2, blocks)),
            dma((2, blocks)),
            dma((ROWS8, TM)),
            dma((ROWS8, TM)),
            dma((2, blocks, TM)),
            dma((2, blocks, TM)),
            dma(()),
            dma(()),
            pltpu.SemaphoreType.REGULAR((SPREAD,)),
            dma((2,)),
            *route_scratch(),
        ],
        compiler_params=pltpu.CompilerParams(
            collective_id=0, has_side_effects=True, vmem_limit_bytes=56 << 20
        ),
        name="first",
    )(taps, raw, dark, flat, gain, labels, lag_row, *tables)


def per_device(
    raw_frames, dark_frame, flat_field, pixel_gain, smoothing_kernel, bin_labels, lag_list
):
    tables = [jnp.asarray(a) for a in dft_tables()]
    sums, most, values, labels = first_round(
        smoothing_kernel, raw_frames, dark_frame, flat_field, pixel_gain, bin_labels,
        lag_list.reshape(1, LAGS), tables,
    )
    needed = most[0, 0]

    def more(state):
        return state[0] < needed

    def again(state):
        step, total = state
        extra, _ = another_round(step.reshape(1, 1), values, labels)
        return step + 1, total + extra

    _, sums = lax.while_loop(more, again, (jnp.int32(1), sums))
    return sums.reshape(-1)[:HALF]


def solution(mesh):
    return jax.shard_map(
        per_device,
        mesh=mesh,
        in_specs=(
            P("tm", "rows", None),
            P("rows", None),
            P("rows", None),
            P("rows", None),
            P(),
            P("rows", None),
            P(),
        ),
        out_specs=P(("rows", "tm")),
        check_vma=False,
    )
```
